32 devices in a mesh: grp: 4 (over y, x), dev: 8 (over z, core).
Axes of the slice: x: 2, y: 2, z: 4, core: 2. Of those that a mesh axis runs over, the one named last changes fastest.
Arguments:
- raw: bfloat16 [128, 16, 4096], P(('grp', 'dev'))
- dark: bfloat16 [16, 4096], replicated, may hold values from 0.049804688 to 0.29882812
- basis: bfloat16 [8, 4096], replicated, may hold values from -3 to 3
- counts: int32 [128], P(('grp', 'dev')), may hold values from 1 to 16, as said below
- positions: int32 [128], replicated, may hold values from 0 to 127, as said below
Outputs:
- corrected: bfloat16 [128, 16, 4096], P(('grp', 'dev'))
- pooled: bfloat16 [4, 16, 1, 30720], P('grp', None, None, 'dev')
The draws below stay inside these ranges and needn't reach their ends.
Inputs may be any that keep to these rules, and one draw needn't show every extreme that they name: `counts`: the first tile of every device (4 tiles in acquisition order) has all 16 planes. A permutation of the tile positions of the slide image. The 4 tiles of the device at grp index g and dev index d lie in 4 different bands, all at tile columns d * 4 to d * 4 + 3.
All inputs are finite; a program needn't handle non-finite values.
Results may differ from the reference program's by a relative error of at most 0.0046.
Values may be sent and summed in bfloat16 or wider, within the bound.
A program may use at most 128 MiB of HBM per device.

```python
import jax
import jax.numpy as jnp
from jax import lax

ROWS = 2
COLS = 2048
OVL = 128
PLANES = 16
RANK = 8
TILES_DEV = 4
TILES = 128
PIX = 4096
BAND = 32
N_GRP = 4
N_DEV = 8


def shading_parts(key):
    basis_key = jax.random.fold_in(key, 11)
    basis = jnp.clip(jax.random.normal(basis_key, (RANK, PIX), jnp.float32), -3.0, 3.0)
    weights = jax.random.normal(jax.random.fold_in(key, 12), (RANK, PLANES), jnp.float32) * 0.1
    drift = jax.random.normal(jax.random.fold_in(key, 13), (RANK, PLANES), jnp.float32) * 0.15
    blocks = TILES // TILES_DEV
    offsets = jax.random.normal(jax.random.fold_in(key, 14), (blocks, RANK, PLANES), jnp.float32) * 0.3
    return (basis, weights, drift, offsets)


def draw_basis(key, part):
    basis, weights, drift, offsets = shading_parts(key)
    return basis.astype(jnp.bfloat16)


def draw_raw(key, part):
    basis, weights, drift, offsets = shading_parts(key)
    blocks = TILES // TILES_DEV
    order = jnp.arange(TILES, dtype=jnp.float32) / TILES
    block_of = jnp.arange(TILES, dtype=jnp.int32) // TILES_DEV
    tile_weights = weights[None] + order[:, None, None] * drift[None] + offsets[block_of]
    shade = jnp.einsum('tkp,kx->tpx', tile_weights, basis)
    block_bright = jnp.exp(jax.random.uniform(jax.random.fold_in(key, 23), (blocks,), jnp.float32, jnp.log(0.3), jnp.log(3.0)))
    rough = jax.random.uniform(jax.random.fold_in(key, 22), (TILES, PLANES, PIX), jnp.float32, 0.5, 1.5)
    bright = 0.4 * jnp.exp(jnp.log(3.0) * order) * jax.random.uniform(jax.random.fold_in(key, 21), (TILES,), jnp.float32, 0.7, 1.4)
    bright = bright * block_bright[block_of]
    values = 0.36 + bright[:, None, None] * rough * jnp.exp(shade)
    return values.astype(jnp.bfloat16)


def draw_counts(key, part):
    drawn = jax.random.randint(jax.random.fold_in(key, 31), (TILES,), 1, PLANES + 1)
    first = jnp.arange(TILES, dtype=jnp.int32) % TILES_DEV == 0
    return jnp.where(first, PLANES, drawn).astype(jnp.int32)


def draw_positions(key, part):
    sources = N_GRP * N_DEV
    band_keys = jax.random.split(jax.random.fold_in(key, 41), sources)
    bands = jax.vmap(lambda k: jax.random.permutation(k, N_GRP))(band_keys).reshape(N_GRP, N_DEV, TILES_DEV)
    slot_keys = jax.random.split(jax.random.fold_in(key, 42), sources)
    slots = jax.vmap(lambda k: jax.random.permutation(k, N_GRP))(slot_keys).reshape(N_GRP, N_DEV, N_GRP)
    column_ids = jnp.arange(N_DEV, dtype=jnp.int32)[None, :, None]
    source_ids = jnp.arange(N_GRP, dtype=jnp.int32)[:, None, None]
    slot = slots[bands, column_ids, source_ids]
    places = bands * BAND + column_ids * TILES_DEV + slot
    return places.reshape(TILES).astype(jnp.int32)


def setup_inputs(seed: int = 0) -> dict:
    key_list = jax.random.split(jax.random.key(seed), 6)
    raw = draw_raw(jax.random.fold_in(key_list[5], 71), 0)
    dark = jnp.clip(jax.random.uniform(key_list[1], (PLANES, PIX), jnp.float32, 0.049804688, 0.29882812), 0.049804688, 0.29882812).astype(jnp.bfloat16)
    basis = draw_basis(jax.random.fold_in(key_list[5], 71), 0)
    counts = draw_counts(jax.random.fold_in(key_list[5], 71), 0)
    positions = draw_positions(jax.random.fold_in(key_list[5], 71), 0)
    return {"raw": raw, "dark": dark, "basis": basis, "counts": counts, "positions": positions}


def feather():
    column = jnp.arange(COLS, dtype=jnp.float32) + 0.5
    return jnp.minimum(1.0, jnp.minimum(column / OVL, (COLS - column) / OVL))


def pooling(tiles):
    count = tiles.shape[0]
    shaped = tiles.reshape(count, PLANES, ROWS, COLS) * feather()
    return jnp.sum(shaped.reshape(count, PLANES, ROWS // 2, 2, COLS // 2, 2), axis=(3, 5)) * 0.25


def reference(raw, dark, basis, counts, positions):
    live = (jnp.arange(PLANES, dtype=jnp.int32)[None, :] < counts[:, None]).astype(jnp.float32)
    blocks = TILES // TILES_DEV
    raw_blocks = raw.reshape(blocks, TILES_DEV, PLANES, PIX)
    live_blocks = live.reshape(blocks, TILES_DEV, PLANES)
    basis_f = basis.astype(jnp.float32)
    dark_f = dark.astype(jnp.float32)

    def gather_terms(carry, item):
        tiles, alive = item
        tiles_f = tiles.astype(jnp.float32)
        projected = jnp.einsum("kx,tpx->tkp", basis_f, tiles_f)
        local_proj = jnp.sum(projected * alive[:, None, :], axis=0)
        local_sum = jnp.sum(jnp.sum(tiles_f, axis=2) * alive, axis=0)
        return (carry[0] + local_proj, carry[1] + local_sum, carry[2] + jnp.sum(alive, axis=0)), None

    start = (jnp.zeros((RANK, PLANES), jnp.float32), jnp.zeros((PLANES,), jnp.float32), jnp.zeros((PLANES,), jnp.float32))
    (proj, total, alive), _ = lax.scan(gather_terms, start, (raw_blocks, live_blocks))
    dark_proj = jnp.dot(basis, dark.T, preferred_element_type=jnp.float32)
    dark_sum = jnp.sum(dark_f, axis=1)
    coef = (proj - alive[None, :] * dark_proj) / (total - alive * dark_sum)[None, :]
    shade = jnp.dot(coef.T, basis_f, precision=lax.Precision.HIGHEST)
    inverse = jnp.exp(-shade)

    def repair(item):
        tiles, alive_rows = item
        return ((tiles.astype(jnp.float32) - dark_f[None]) * inverse[None] * alive_rows[:, :, None]).astype(jnp.bfloat16)

    corrected = lax.map(repair, (raw_blocks, live_blocks)).reshape(TILES, PLANES, PIX)
    order = jnp.argsort(positions).astype(jnp.int32)
    half_step = (COLS - OVL) // 2
    half_ovl = OVL // 2

    def band_rows(band):
        chosen = lax.dynamic_slice_in_dim(order, band * BAND, BAND)
        cells = pooling(corrected[chosen].astype(jnp.float32)).astype(jnp.bfloat16)
        cells = lax.optimization_barrier(cells)
        head = cells[..., :half_step].astype(jnp.float32)
        tail = cells[..., half_step:]
        carried = jnp.concatenate([jnp.zeros_like(tail[:1]), tail[:-1]], axis=0)
        carried = jnp.pad(carried, ((0, 0), (0, 0), (0, 0), (0, half_step - half_ovl))).astype(jnp.float32)
        merged = head + carried
        return jnp.transpose(merged, (1, 2, 0, 3)).reshape(PLANES, ROWS // 2, BAND * half_step).astype(jnp.bfloat16)

    pooled = lax.map(band_rows, jnp.arange(N_GRP, dtype=jnp.int32))
    return corrected, pooled
```

```python
import functools

import jax
import jax.numpy as jnp
from jax import lax
from jax.experimental import pallas as pl
from jax.experimental.pallas import tpu as pltpu
from jax.sharding import PartitionSpec as P

ROWS = 2
COLS = 2048
OVL = 128
LANES = 128
BLOCK = 256
MESH = pl.DeviceIdType.MESH
NT = (((1,), (1,)), ((), ()))


def pool_weights(block, blocks):
    row = lax.broadcasted_iota(jnp.int32, (BLOCK, LANES), 0)
    lane = lax.broadcasted_iota(jnp.int32, (BLOCK, LANES), 1)
    column = (row + block * BLOCK).astype(jnp.float32) + 0.5
    ramp = jnp.minimum(1.0, jnp.minimum(column / OVL, (blocks * BLOCK - column) / OVL))
    inside = (row >= 2 * lane) & (row < 2 * lane + 2)
    return jnp.where(inside, 0.25 * ramp, 0.0).astype(jnp.bfloat16)


def kernel(
    groups, columns,
    counts_ref, positions_ref, raw_ref, dark_ref, basis_ref,
    corrected_ref, pooled_ref,
    rhs, stat, grp_buf, dev_buf, weights, outgoing, arrived, tail_out, tail_in, acc,
    grp_send, grp_recv, dev_send, dev_recv, cell_send, cell_recv, tail_send, tail_recv,
):
    tiles, planes, pixels = raw_ref.shape
    rank = basis_ref.shape[0]
    band_size = columns * tiles
    half_step = (COLS - OVL) // 2
    half_ovl = OVL // 2
    cells_wide = COLS // 2
    last = cells_wide - LANES
    blocks = COLS // BLOCK
    g = lax.axis_index("grp")
    d = lax.axis_index("dev")

    barrier = pltpu.get_barrier_semaphore()
    near = [lax.rem(d + 1, columns), lax.rem(d + columns - 1, columns)]
    for o in range(1, groups):
        other = lax.rem(g + o, groups)
        for where in [d] + near:
            pl.semaphore_signal(barrier, inc=1, device_id=(other, where), device_id_type=MESH)
    for o in range(1, columns):
        pl.semaphore_signal(
            barrier, inc=1, device_id=(g, lax.rem(d + o, columns)), device_id_type=MESH
        )

    rhs[0:rank, :] = basis_ref[...]
    rhs[rank:, :] = jnp.ones((rhs.shape[0] - rank, pixels), jnp.bfloat16)
    width = rhs.shape[0]
    sums = lax.dot_general(
        raw_ref[...].reshape(tiles * planes, pixels), rhs[...], NT,
        preferred_element_type=jnp.float32,
    )
    dark_sums = lax.dot_general(dark_ref[...], rhs[...], NT, preferred_element_type=jnp.float32)
    plane = lax.broadcasted_iota(jnp.int32, (planes, width), 0)
    local = jnp.zeros((planes, width), jnp.float32)
    for t in range(tiles):
        part = sums[t * planes:(t + 1) * planes] - dark_sums
        local = local + jnp.where(plane < counts_ref[t], part, 0.0)
    stat[...] = jnp.zeros_like(stat)
    stat[:, 0:width] = local
    half = planes // 2
    grp_buf[g] = stat[0:half, :] + pltpu.roll(stat[half:, :], LANES // 2, 1)

    pl.semaphore_wait(barrier, 3 * (groups - 1) + columns - 1)

    copies = []
    for o in range(1, groups):
        other = lax.rem(g + o, groups)
        copy = pltpu.make_async_remote_copy(
            src_ref=grp_buf.at[g], dst_ref=grp_buf.at[g],
            send_sem=grp_send.at[o], recv_sem=grp_recv.at[g],
            device_id=(other, d), device_id_type=MESH,
        )
        copy.start()
        copies.append(copy)
    weights[0] = pool_weights(0, blocks)
    weights[1] = pool_weights(1, blocks)
    weights[2] = pool_weights(blocks - 1, blocks)
    for o in range(1, groups):
        source = lax.rem(g + groups - o, groups)
        pltpu.make_async_remote_copy(
            src_ref=grp_buf.at[source], dst_ref=grp_buf.at[source],
            send_sem=grp_send.at[o], recv_sem=grp_recv.at[source],
            device_id=(source, d), device_id_type=MESH,
        ).wait_recv()
    for copy in copies:
        copy.wait_send()
    dev_buf[d] = jnp.sum(grp_buf[...], axis=0)
    copies = []
    for o in range(1, columns):
        copy = pltpu.make_async_remote_copy(
            src_ref=dev_buf.at[d], dst_ref=dev_buf.at[d],
            send_sem=dev_send.at[o], recv_sem=dev_recv.at[d],
            device_id=(g, lax.rem(d + o, columns)), device_id_type=MESH,
        )
        copy.start()
        copies.append(copy)
    for o in range(1, columns):
        source = lax.rem(d + columns - o, columns)
        pltpu.make_async_remote_copy(
            src_ref=dev_buf.at[source], dst_ref=dev_buf.at[source],
            send_sem=dev_send.at[o], recv_sem=dev_recv.at[source],
            device_id=(g, source), device_id_type=MESH,
        ).wait_recv()
    for copy in copies:
        copy.wait_send()
    packed = jnp.sum(dev_buf[...], axis=0)
    full = jnp.concatenate([packed, pltpu.roll(packed, LANES // 2, 1)], axis=0)
    coef = full[:, 0:rank] / full[:, rank:rank + 1]
    high = coef.astype(jnp.bfloat16)
    rest = coef - high.astype(jnp.float32)
    middle = rest.astype(jnp.bfloat16)
    low = (rest - middle.astype(jnp.float32)).astype(jnp.bfloat16)
    basis = basis_ref[...]
    shade = (
        jnp.dot(low, basis, preferred_element_type=jnp.float32)
        + jnp.dot(middle, basis, preferred_element_type=jnp.float32)
        + jnp.dot(high, basis, preferred_element_type=jnp.float32)
    )
    inverse = jnp.exp(-shade)
    dark = dark_ref[...].astype(jnp.float32)
    plane = lax.broadcasted_iota(jnp.int32, (planes, pixels), 0)
    for t in range(tiles):
        fixed = (raw_ref[t].astype(jnp.float32) - dark) * inverse
        corrected_ref[t] = jnp.where(plane < counts_ref[t], fixed, 0.0).astype(jnp.bfloat16)

    pieces = []
    for block in range(blocks):
        kind = 0 if block == 0 else 2 if block == blocks - 1 else 1
        total = None
        for row in range(ROWS):
            start = row * COLS + block * BLOCK
            part = jnp.dot(
                corrected_ref[:, :, start:start + BLOCK].reshape(tiles * planes, BLOCK),
                weights[kind],
                preferred_element_type=jnp.float32,
            )
            total = part if total is None else total + part
        pieces.append(total)
    cells = jnp.concatenate(pieces, axis=1)

    mine = (g * columns + d) * tiles
    place = [positions_ref[mine + t] for t in range(tiles)]
    for b in range(groups):
        chosen = jnp.zeros((planes, cells_wide), jnp.float32)
        tail = jnp.zeros((planes, LANES), jnp.float32)
        for t in range(tiles):
            rows = cells[t * planes:(t + 1) * planes]
            band = jnp.full((planes, cells_wide), lax.div(place[t], band_size), jnp.int32)
            chosen = jnp.where(band == b, rows, chosen)
            ends = jnp.full((planes, LANES), place[t], jnp.int32)
            final = jnp.full((planes, LANES), lax.rem(place[t], tiles), jnp.int32)
            hit = (ends >= b * band_size) & (ends < (b + 1) * band_size) & (final == tiles - 1)
            tail = jnp.where(hit, rows[:, last:], tail)
        outgoing[b] = chosen.astype(jnp.bfloat16)
        tail_out[b] = tail.astype(jnp.bfloat16)

    def cell_copy(o):
        other = lax.rem(g + o, groups)
        return pltpu.make_async_remote_copy(
            src_ref=outgoing.at[other], dst_ref=arrived.at[g],
            send_sem=cell_send.at[o], recv_sem=cell_recv.at[g],
            device_id=(other, d), device_id_type=MESH,
        )

    def tail_copy(o):
        other = lax.rem(g + o, groups)
        return pltpu.make_async_remote_copy(
            src_ref=tail_out.at[other], dst_ref=tail_in.at[g],
            send_sem=tail_send.at[o], recv_sem=tail_recv.at[g],
            device_id=(other, lax.rem(d + 1, columns)), device_id_type=MESH,
        )

    for o in range(1, groups):
        cell_copy(o).start()

    @pl.when(d < columns - 1)
    def _():
        for o in range(groups):
            tail_copy(o).start()

    acc[...] = jnp.zeros_like(acc)
    arrived[g] = outgoing[g]
    for o in range(1, groups):
        source = lax.rem(g + groups - o, groups)
        pltpu.make_async_remote_copy(
            src_ref=outgoing.at[source], dst_ref=arrived.at[source],
            send_sem=cell_send.at[o], recv_sem=cell_recv.at[source],
            device_id=(source, d), device_id_type=MESH,
        ).wait_recv()
    slots = []
    for source in range(groups):
        slot = jnp.int32(0)
        for t in range(tiles):
            at = positions_ref[(source * columns + d) * tiles + t]
            slot = slot + jnp.where(lax.div(at, band_size) == g, lax.rem(at, tiles), 0)
        slots.append(slot)
    for j in range(tiles):
        cell = jnp.zeros((planes, cells_wide), jnp.float32)
        for source in range(groups):
            here = jnp.full((planes, cells_wide), slots[source], jnp.int32) == j
            cell = jnp.where(here, arrived[source].astype(jnp.float32), cell)
        base, shift = divmod(j * half_step, LANES)
        base = base * LANES
        if shift:
            cell = jnp.concatenate([cell, jnp.zeros((planes, LANES), jnp.float32)], axis=1)
            cell = pltpu.roll(cell, shift, 1)
        acc[:, base:base + cell.shape[1]] += cell

    @pl.when(d > 0)
    def _():
        spill = jnp.zeros((planes, LANES), jnp.float32)
        for o in range(groups):
            source = lax.rem(g + groups - o, groups)
            pltpu.make_async_remote_copy(
                src_ref=tail_out.at[source], dst_ref=tail_in.at[source],
                send_sem=tail_send.at[o], recv_sem=tail_recv.at[source],
                device_id=(source, lax.rem(d + columns - 1, columns)), device_id_type=MESH,
            ).wait_recv()
        for source in range(groups):
            spill = spill + tail_in[source].astype(jnp.float32)
        spill = pltpu.roll(spill, half_ovl, 1)
        lane = lax.broadcasted_iota(jnp.int32, (planes, LANES), 1)
        acc[:, 0:LANES] += jnp.where(lane < half_ovl, spill, 0.0)

    pooled_ref[...] = acc[:, 0:tiles * half_step].astype(jnp.bfloat16)
    for o in range(1, groups):
        cell_copy(o).wait_send()

    @pl.when(d < columns - 1)
    def _():
        for o in range(groups):
            tail_copy(o).wait_send()


def per_device(groups, columns, raw, dark, basis, counts, positions):
    tiles, planes, pixels = raw.shape
    half_step = (COLS - OVL) // 2
    bf16, f32 = jnp.bfloat16, jnp.float32
    vmem = pl.BlockSpec(memory_space=pltpu.VMEM)
    smem = pl.BlockSpec(memory_space=pltpu.SMEM)
    dma = pltpu.SemaphoreType.DMA
    corrected, pooled = pl.pallas_call(
        functools.partial(kernel, groups, columns),
        out_shape=(
            jax.ShapeDtypeStruct(raw.shape, bf16),
            jax.ShapeDtypeStruct((planes, tiles * half_step), bf16),
        ),
        in_specs=[smem, smem, vmem, vmem, vmem],
        out_specs=(vmem, vmem),
        scratch_shapes=[
            pltpu.VMEM((16, pixels), bf16),
            pltpu.VMEM((planes, LANES), f32),
            pltpu.VMEM((groups, planes // 2, LANES), f32),
            pltpu.VMEM((columns, planes // 2, LANES), f32),
            pltpu.VMEM((3, BLOCK, LANES), bf16),
            pltpu.VMEM((groups, planes, COLS // 2), bf16),
            pltpu.VMEM((groups, planes, COLS // 2), bf16),
            pltpu.VMEM((groups, planes, LANES), bf16),
            pltpu.VMEM((groups, planes, LANES), bf16),
            pltpu.VMEM((planes, tiles * half_step + LANES), f32),
            dma((groups,)), dma((groups,)), dma((columns,)), dma((columns,)),
            dma((groups,)), dma((groups,)), dma((groups,)), dma((groups,)),
        ],
        compiler_params=pltpu.CompilerParams(collective_id=0, has_side_effects=True),
    )(counts, positions, raw, dark, basis)
    return corrected, pooled.reshape(1, planes, ROWS // 2, tiles * half_step)


def solution(mesh):
    in_specs = (P(("grp", "dev"), None, None), P(), P(), P(("grp", "dev")), P())
    out_specs = (P(("grp", "dev"), None, None), P("grp", None, None, "dev"))
    return jax.shard_map(
        functools.partial(per_device, mesh.shape["grp"], mesh.shape["dev"]),
        mesh=mesh, in_specs=in_specs, out_specs=out_specs, check_vma=False,
    )
```

```python
import functools

import jax
import jax.numpy as jnp
from jax import lax
from jax.experimental import pallas as pl
from jax.experimental.pallas import tpu as pltpu
from jax.sharding import PartitionSpec as P

ROWS = 2
COLS = 2048
OVL = 128
LANES = 128
BLOCK = 256
MESH = pl.DeviceIdType.MESH
NT = (((1,), (1,)), ((), ()))


def pool_weights(block, blocks):
    row = lax.broadcasted_iota(jnp.int32, (BLOCK, LANES), 0)
    lane = lax.broadcasted_iota(jnp.int32, (BLOCK, LANES), 1)
    column = (row + block * BLOCK).astype(jnp.float32) + 0.5
    ramp = jnp.minimum(1.0, jnp.minimum(column / OVL, (blocks * BLOCK - column) / OVL))
    inside = (row >= 2 * lane) & (row < 2 * lane + 2)
    return jnp.where(inside, 0.25 * ramp, 0.0).astype(jnp.bfloat16)


def kernel(
    groups, columns,
    counts_hbm, positions_hbm, raw_hbm, dark_hbm, basis_hbm,
    corrected_hbm, pooled_ref,
    counts_ref, positions_ref, raw_ref, dark_ref, rhs, corrected_ref,
    stat, grp_buf, dev_buf, weights, outgoing, arrived, tail_out, tail_in, acc,
    in_sem, raw_sem, out_sem,
    grp_send, grp_recv, dev_send, dev_recv, cell_send, cell_recv, tail_send, tail_recv,
):
    tiles, planes, pixels = raw_ref.shape
    rank = basis_hbm.shape[0]
    band_size = columns * tiles
    half_step = (COLS - OVL) // 2
    half_ovl = OVL // 2
    cells_wide = COLS // 2
    blocks = COLS // BLOCK
    g = lax.axis_index("grp")
    d = lax.axis_index("dev")

    raw_loads = [
        pltpu.make_async_copy(raw_hbm.at[t], raw_ref.at[t], raw_sem.at[t]) for t in range(tiles)
    ]
    loads = [
        pltpu.make_async_copy(basis_hbm, rhs.at[0:rank], in_sem.at[0]),
        pltpu.make_async_copy(dark_hbm, dark_ref, in_sem.at[1]),
        pltpu.make_async_copy(counts_hbm, counts_ref, in_sem.at[2]),
        pltpu.make_async_copy(positions_hbm, positions_ref, in_sem.at[3]),
    ]
    for copy in loads[:2] + raw_loads + loads[2:]:
        copy.start()

    barrier = pltpu.get_barrier_semaphore()
    near = [lax.rem(d + 1, columns), lax.rem(d + columns - 1, columns)]
    for o in range(1, groups):
        other = lax.rem(g + o, groups)
        for where in [d] + near:
            pl.semaphore_signal(barrier, inc=1, device_id=(other, where), device_id_type=MESH)
    for o in range(1, columns):
        pl.semaphore_signal(
            barrier, inc=1, device_id=(g, lax.rem(d + o, columns)), device_id_type=MESH
        )

    rhs[rank:, :] = jnp.ones((rhs.shape[0] - rank, pixels), jnp.bfloat16)
    width = rhs.shape[0]
    weights[0] = pool_weights(0, blocks)
    weights[1] = pool_weights(1, blocks)
    weights[2] = pool_weights(blocks - 1, blocks)
    stat[...] = jnp.zeros_like(stat)
    for copy in loads:
        copy.wait()
    dark_sums = lax.dot_general(dark_ref[...], rhs[...], NT, preferred_element_type=jnp.float32)
    plane = lax.broadcasted_iota(jnp.int32, (planes, width), 0)
    for copy in raw_loads:
        copy.wait()
    sums = lax.dot_general(
        raw_ref[...].reshape(tiles * planes, pixels), rhs[...], NT,
        preferred_element_type=jnp.float32,
    )
    local = jnp.zeros((planes, width), jnp.float32)
    for t in range(tiles):
        part = sums[t * planes:(t + 1) * planes] - dark_sums
        local = local + jnp.where(plane < counts_ref[t], part, 0.0)
    stat[:, 0:width] = local
    half = planes // 2
    grp_buf[g] = stat[0:half, :] + pltpu.roll(stat[half:, :], LANES // 2, 1)

    pl.semaphore_wait(barrier, 3 * (groups - 1) + columns - 1)

    sent = []
    for o in range(1, groups):
        other = lax.rem(g + o, groups)
        copy = pltpu.make_async_remote_copy(
            src_ref=grp_buf.at[g], dst_ref=grp_buf.at[g],
            send_sem=grp_send.at[o], recv_sem=grp_recv.at[g],
            device_id=(other, d), device_id_type=MESH,
        )
        copy.start()
        sent.append(copy)
    for o in range(1, groups):
        source = lax.rem(g + groups - o, groups)
        pltpu.make_async_remote_copy(
            src_ref=grp_buf.at[source], dst_ref=grp_buf.at[source],
            send_sem=grp_send.at[o], recv_sem=grp_recv.at[source],
            device_id=(source, d), device_id_type=MESH,
        ).wait_recv()
    dev_buf[d] = jnp.sum(grp_buf[...], axis=0)
    for o in range(1, columns):
        copy = pltpu.make_async_remote_copy(
            src_ref=dev_buf.at[d], dst_ref=dev_buf.at[d],
            send_sem=dev_send.at[o], recv_sem=dev_recv.at[d],
            device_id=(g, lax.rem(d + o, columns)), device_id_type=MESH,
        )
        copy.start()
        sent.append(copy)
    acc[...] = jnp.zeros_like(acc)
    for o in range(1, columns):
        source = lax.rem(d + columns - o, columns)
        pltpu.make_async_remote_copy(
            src_ref=dev_buf.at[source], dst_ref=dev_buf.at[source],
            send_sem=dev_send.at[o], recv_sem=dev_recv.at[source],
            device_id=(g, source), device_id_type=MESH,
        ).wait_recv()
    packed = jnp.sum(dev_buf[...], axis=0)
    full = jnp.concatenate([packed, pltpu.roll(packed, LANES // 2, 1)], axis=0)
    coef = full[:, 0:rank] / full[:, rank:rank + 1]
    high = coef.astype(jnp.bfloat16)
    rest = coef - high.astype(jnp.float32)
    middle = rest.astype(jnp.bfloat16)
    low = (rest - middle.astype(jnp.float32)).astype(jnp.bfloat16)

    mine = (g * columns + d) * tiles
    place = [positions_ref[mine + t] for t in range(tiles)]
    band_of = [jnp.full((planes, LANES), lax.div(p, band_size), jnp.int32) for p in place]
    slot_of = [jnp.full((planes, LANES), lax.rem(p, tiles), jnp.int32) for p in place]
    plane = lax.broadcasted_iota(jnp.int32, (planes, BLOCK), 0)
    live = [plane < counts_ref[t] for t in range(tiles)]
    for block in range(blocks):
        kind = 0 if block == 0 else 2 if block == blocks - 1 else 1
        total = None
        for row in range(ROWS):
            span = slice(row * COLS + block * BLOCK, row * COLS + (block + 1) * BLOCK)
            basis = rhs[0:rank, span]
            shade = (
                jnp.dot(low, basis, preferred_element_type=jnp.float32)
                + jnp.dot(middle, basis, preferred_element_type=jnp.float32)
                + jnp.dot(high, basis, preferred_element_type=jnp.float32)
            )
            inverse = jnp.exp(-shade)
            dark = dark_ref[:, span].astype(jnp.float32)
            made = []
            for t in range(tiles):
                fixed = (raw_ref[t, :, span].astype(jnp.float32) - dark) * inverse
                fixed = jnp.where(live[t], fixed, 0.0).astype(jnp.bfloat16)
                corrected_ref[t, :, span] = fixed
                made.append(fixed)
            part = jnp.dot(
                jnp.concatenate(made, axis=0), weights[kind], preferred_element_type=jnp.float32
            )
            total = part if total is None else total + part
        lanes = slice(block * LANES, (block + 1) * LANES)
        rows = [total[t * planes:(t + 1) * planes] for t in range(tiles)]
        for b in range(groups):
            chosen = jnp.zeros((planes, LANES), jnp.float32)
            tail = jnp.zeros((planes, LANES), jnp.float32)
            for t in range(tiles):
                hit = band_of[t] == b
                chosen = jnp.where(hit, rows[t], chosen)
                if block == blocks - 1:
                    tail = jnp.where(hit & (slot_of[t] == tiles - 1), rows[t], tail)
            outgoing[b, :, lanes] = chosen.astype(jnp.bfloat16)
            if block == blocks - 1:
                tail_out[b] = tail.astype(jnp.bfloat16)

    def cell_copy(o):
        other = lax.rem(g + o, groups)
        return pltpu.make_async_remote_copy(
            src_ref=outgoing.at[other], dst_ref=arrived.at[g],
            send_sem=cell_send.at[o], recv_sem=cell_recv.at[g],
            device_id=(other, d), device_id_type=MESH,
        )

    def tail_copy(o):
        other = lax.rem(g + o, groups)
        return pltpu.make_async_remote_copy(
            src_ref=tail_out.at[other], dst_ref=tail_in.at[g],
            send_sem=tail_send.at[o], recv_sem=tail_recv.at[g],
            device_id=(other, lax.rem(d + 1, columns)), device_id_type=MESH,
        )

    for o in range(1, groups):
        cell_copy(o).start()

    @pl.when(d < columns - 1)
    def _():
        for o in range(groups):
            tail_copy(o).start()

    stores = [
        pltpu.make_async_copy(corrected_ref.at[t], corrected_hbm.at[t], out_sem.at[t])
        for t in range(tiles)
    ]
    for copy in stores:
        copy.start()
    arrived[g] = outgoing[g]
    for o in range(1, groups):
        source = lax.rem(g + groups - o, groups)
        pltpu.make_async_remote_copy(
            src_ref=outgoing.at[source], dst_ref=arrived.at[source],
            send_sem=cell_send.at[o], recv_sem=cell_recv.at[source],
            device_id=(source, d), device_id_type=MESH,
        ).wait_recv()
    slots = []
    for source in range(groups):
        slot = jnp.int32(0)
        for t in range(tiles):
            at = positions_ref[(source * columns + d) * tiles + t]
            slot = slot + jnp.where(lax.div(at, band_size) == g, lax.rem(at, tiles), 0)
        slots.append(slot)
    for j in range(tiles):
        cell = jnp.zeros((planes, cells_wide), jnp.float32)
        for source in range(groups):
            here = jnp.full((planes, cells_wide), slots[source], jnp.int32) == j
            cell = jnp.where(here, arrived[source].astype(jnp.float32), cell)
        base, shift = divmod(j * half_step, LANES)
        base = base * LANES
        if shift:
            cell = jnp.concatenate([cell, jnp.zeros((planes, LANES), jnp.float32)], axis=1)
            cell = pltpu.roll(cell, shift, 1)
        acc[:, base:base + cell.shape[1]] += cell

    @pl.when(d > 0)
    def _():
        spill = jnp.zeros((planes, LANES), jnp.float32)
        for o in range(groups):
            source = lax.rem(g + groups - o, groups)
            pltpu.make_async_remote_copy(
                src_ref=tail_out.at[source], dst_ref=tail_in.at[source],
                send_sem=tail_send.at[o], recv_sem=tail_recv.at[source],
                device_id=(source, lax.rem(d + columns - 1, columns)), device_id_type=MESH,
            ).wait_recv()
        for source in range(groups):
            spill = spill + tail_in[source].astype(jnp.float32)
        spill = pltpu.roll(spill, half_ovl, 1)
        lane = lax.broadcasted_iota(jnp.int32, (planes, LANES), 1)
        acc[:, 0:LANES] += jnp.where(lane < half_ovl, spill, 0.0)

    pooled_ref[...] = acc[:, 0:tiles * half_step].astype(jnp.bfloat16)
    for copy in sent:
        copy.wait_send()
    for copy in stores:
        copy.wait()
    for o in range(1, groups):
        cell_copy(o).wait_send()

    @pl.when(d < columns - 1)
    def _():
        for o in range(groups):
            tail_copy(o).wait_send()


def per_device(groups, columns, raw, dark, basis, counts, positions):
    tiles, planes, pixels = raw.shape
    half_step = (COLS - OVL) // 2
    bf16, f32 = jnp.bfloat16, jnp.float32
    vmem = pl.BlockSpec(memory_space=pltpu.VMEM)
    anywhere = pl.BlockSpec(memory_space=pl.ANY)
    dma = pltpu.SemaphoreType.DMA
    corrected, pooled = pl.pallas_call(
        functools.partial(kernel, groups, columns),
        out_shape=(
            jax.ShapeDtypeStruct(raw.shape, bf16),
            jax.ShapeDtypeStruct((planes, tiles * half_step), bf16),
        ),
        in_specs=[anywhere] * 5,
        out_specs=(anywhere, vmem),
        scratch_shapes=[
            pltpu.SMEM(counts.shape, jnp.int32),
            pltpu.SMEM(positions.shape, jnp.int32),
            pltpu.VMEM(raw.shape, bf16),
            pltpu.VMEM(dark.shape, bf16),
            pltpu.VMEM((16, pixels), bf16),
            pltpu.VMEM(raw.shape, bf16),
            pltpu.VMEM((planes, LANES), f32),
            pltpu.VMEM((groups, planes // 2, LANES), f32),
            pltpu.VMEM((columns, planes // 2, LANES), f32),
            pltpu.VMEM((3, BLOCK, LANES), bf16),
            pltpu.VMEM((groups, planes, COLS // 2), bf16),
            pltpu.VMEM((groups, planes, COLS // 2), bf16),
            pltpu.VMEM((groups, planes, LANES), bf16),
            pltpu.VMEM((groups, planes, LANES), bf16),
            pltpu.VMEM((planes, tiles * half_step + LANES), f32),
            dma((4,)), dma((tiles,)), dma((tiles,)),
            dma((groups,)), dma((groups,)), dma((columns,)), dma((columns,)),
            dma((groups,)), dma((groups,)), dma((groups,)), dma((groups,)),
        ],
        compiler_params=pltpu.CompilerParams(
            collective_id=0, has_side_effects=True, vmem_limit_bytes=16 << 20
        ),
    )(*[pltpu.with_memory_space_constraint(x, pltpu.HBM) for x in (counts, positions, raw, dark, basis)])
    return corrected, pooled.reshape(1, planes, ROWS // 2, tiles * half_step)


def solution(mesh):
    in_specs = (P(("grp", "dev"), None, None), P(), P(), P(("grp", "dev")), P())
    out_specs = (P(("grp", "dev"), None, None), P("grp", None, None, "dev"))
    return jax.shard_map(
        functools.partial(per_device, mesh.shape["grp"], mesh.shape["dev"]),
        mesh=mesh, in_specs=in_specs, out_specs=out_specs, check_vma=False,
    )
```

```python
import functools

import jax
import jax.numpy as jnp
from jax import lax
from jax.experimental import pallas as pl
from jax.experimental.pallas import tpu as pltpu
from jax.sharding import PartitionSpec as P

ROWS = 2
COLS = 2048
OVL = 128
LANES = 128
BLOCK = 256
MESH = pl.DeviceIdType.MESH
NT = (((1,), (1,)), ((), ()))


def pick(options):
    found = jnp.int32(0)
    for hit, value in options:
        found = jnp.where(hit, value, found)
    return found


def pool_weights(block, blocks):
    row = lax.broadcasted_iota(jnp.int32, (BLOCK, LANES), 0)
    lane = lax.broadcasted_iota(jnp.int32, (BLOCK, LANES), 1)
    column = (row + block * BLOCK).astype(jnp.float32) + 0.5
    ramp = jnp.minimum(1.0, jnp.minimum(column / OVL, (blocks * BLOCK - column) / OVL))
    inside = (row >= 2 * lane) & (row < 2 * lane + 2)
    return jnp.where(inside, 0.25 * ramp, 0.0).astype(jnp.bfloat16)


def kernel(
    groups, columns,
    counts_hbm, positions_hbm, raw_hbm, dark_hbm, basis_hbm,
    corrected_hbm, pooled_ref,
    counts_ref, positions_ref, raw_ref, dark_ref, rhs, corrected_ref,
    stat, grp_buf, dev_buf, weights, outgoing, arrived, tail_out, tail_in, inverse_ref, placed, acc,
    in_sem, raw_sem, out_sem,
    grp_send, grp_recv, dev_send, dev_recv, cell_send, cell_recv, tail_send, tail_recv,
):
    tiles, planes, pixels = raw_ref.shape
    rank = basis_hbm.shape[0]
    band_size = columns * tiles
    half_step = (COLS - OVL) // 2
    half_ovl = OVL // 2
    blocks = COLS // BLOCK
    g = lax.axis_index("grp")
    d = lax.axis_index("dev")

    raw_loads = [
        pltpu.make_async_copy(raw_hbm.at[t], raw_ref.at[t], raw_sem.at[t]) for t in range(tiles)
    ]
    loads = [
        pltpu.make_async_copy(basis_hbm, rhs.at[0:rank], in_sem.at[0]),
        pltpu.make_async_copy(dark_hbm, dark_ref, in_sem.at[1]),
        pltpu.make_async_copy(counts_hbm, counts_ref, in_sem.at[2]),
        pltpu.make_async_copy(positions_hbm, positions_ref, in_sem.at[3]),
    ]
    for copy in loads[:2] + raw_loads + loads[2:]:
        copy.start()

    barrier = pltpu.get_barrier_semaphore()
    near = [lax.rem(d + 1, columns), lax.rem(d + columns - 1, columns)]
    for o in range(1, groups):
        other = lax.rem(g + o, groups)
        for where in [d] + near:
            pl.semaphore_signal(barrier, inc=1, device_id=(other, where), device_id_type=MESH)
    for o in range(1, columns):
        pl.semaphore_signal(
            barrier, inc=1, device_id=(g, lax.rem(d + o, columns)), device_id_type=MESH
        )

    rhs[rank:, :] = jnp.ones((rhs.shape[0] - rank, pixels), jnp.bfloat16)
    width = rhs.shape[0]
    weights[0] = pool_weights(0, blocks)
    weights[1] = pool_weights(1, blocks)
    weights[2] = pool_weights(blocks - 1, blocks)
    stat[...] = jnp.zeros_like(stat)
    for copy in loads:
        copy.wait()
    dark_sums = lax.dot_general(dark_ref[...], rhs[...], NT, preferred_element_type=jnp.float32)
    plane = lax.broadcasted_iota(jnp.int32, (planes, width), 0)
    for copy in raw_loads:
        copy.wait()
    sums = lax.dot_general(
        raw_ref[...].reshape(tiles * planes, pixels), rhs[...], NT,
        preferred_element_type=jnp.float32,
    )
    local = jnp.zeros((planes, width), jnp.float32)
    for t in range(tiles):
        part = sums[t * planes:(t + 1) * planes] - dark_sums
        local = local + jnp.where(plane < counts_ref[t], part, 0.0)
    stat[:, 0:width] = local
    half = planes // 2
    grp_buf[g] = stat[0:half, :] + pltpu.roll(stat[half:, :], LANES // 2, 1)

    def home(at):
        return lax.div(at, band_size), lax.rem(at, tiles)

    wide = lax.broadcasted_iota(jnp.int32, (planes, pixels), 0)
    mine = [home(positions_ref[(g * columns + d) * tiles + t]) for t in range(tiles)]
    for b in range(groups):
        chosen = pick((mine[t][0] == b, t) for t in range(tiles))
        masked = jnp.where(
            wide < counts_ref[chosen],
            raw_ref[chosen].astype(jnp.float32), dark_ref[...].astype(jnp.float32),
        ).astype(jnp.bfloat16)
        outgoing[b] = masked
        for row in range(ROWS):
            tail_out[b, row] = masked[:, (row + 1) * COLS - OVL:(row + 1) * COLS]
    arrived[g] = outgoing[g]

    pl.semaphore_wait(barrier, 3 * (groups - 1) + columns - 1)

    sent = []
    for o in range(1, groups):
        other = lax.rem(g + o, groups)
        copy = pltpu.make_async_remote_copy(
            src_ref=grp_buf.at[g], dst_ref=grp_buf.at[g],
            send_sem=grp_send.at[o], recv_sem=grp_recv.at[g],
            device_id=(other, d), device_id_type=MESH,
        )
        copy.start()
        sent.append(copy)

    def cell_copy(o):
        other = lax.rem(g + o, groups)
        return pltpu.make_async_remote_copy(
            src_ref=outgoing.at[other], dst_ref=arrived.at[g],
            send_sem=cell_send.at[o], recv_sem=cell_recv.at[g],
            device_id=(other, d), device_id_type=MESH,
        )

    def tail_copy(o):
        other = lax.rem(g + o, groups)
        return pltpu.make_async_remote_copy(
            src_ref=tail_out.at[other], dst_ref=tail_in.at[g],
            send_sem=tail_send.at[o], recv_sem=tail_recv.at[g],
            device_id=(other, lax.rem(d + 1, columns)), device_id_type=MESH,
        )

    @pl.when(d < columns - 1)
    def _():
        for o in range(groups):
            tail_copy(o).start()

    for o in range(1, groups):
        cell_copy(o).start()

    for o in range(1, groups):
        source = lax.rem(g + groups - o, groups)
        pltpu.make_async_remote_copy(
            src_ref=grp_buf.at[source], dst_ref=grp_buf.at[source],
            send_sem=grp_send.at[o], recv_sem=grp_recv.at[source],
            device_id=(source, d), device_id_type=MESH,
        ).wait_recv()
    dev_buf[d] = jnp.sum(grp_buf[...], axis=0)
    for o in range(1, columns):
        copy = pltpu.make_async_remote_copy(
            src_ref=dev_buf.at[d], dst_ref=dev_buf.at[d],
            send_sem=dev_send.at[o], recv_sem=dev_recv.at[d],
            device_id=(g, lax.rem(d + o, columns)), device_id_type=MESH,
        )
        copy.start()
        sent.append(copy)
    acc[...] = jnp.zeros_like(acc)
    for o in range(1, columns):
        source = lax.rem(d + columns - o, columns)
        pltpu.make_async_remote_copy(
            src_ref=dev_buf.at[source], dst_ref=dev_buf.at[source],
            send_sem=dev_send.at[o], recv_sem=dev_recv.at[source],
            device_id=(g, source), device_id_type=MESH,
        ).wait_recv()
    packed = jnp.sum(dev_buf[...], axis=0)
    full = jnp.concatenate([packed, pltpu.roll(packed, LANES // 2, 1)], axis=0)
    coef = full[:, 0:rank] / full[:, rank:rank + 1]
    high = coef.astype(jnp.bfloat16)
    rest = coef - high.astype(jnp.float32)
    middle = rest.astype(jnp.bfloat16)
    low = (rest - middle.astype(jnp.float32)).astype(jnp.bfloat16)

    parts = jnp.concatenate([low, middle, high], axis=1)
    plane = lax.broadcasted_iota(jnp.int32, (planes, BLOCK), 0)
    live = [plane < counts_ref[t] for t in range(tiles)]
    for block in range(pixels // BLOCK):
        span = slice(block * BLOCK, (block + 1) * BLOCK)
        basis = rhs[0:rank, span]
        shade = jnp.dot(
            parts, jnp.concatenate([basis, basis, basis], axis=0),
            preferred_element_type=jnp.float32,
        )
        inverse = jnp.exp(-shade)
        inverse_ref[:, span] = inverse
        dark = dark_ref[:, span].astype(jnp.float32)
        for t in range(tiles):
            fixed = (raw_ref[t, :, span].astype(jnp.float32) - dark) * inverse
            corrected_ref[t, :, span] = jnp.where(live[t], fixed, 0.0).astype(jnp.bfloat16)

    stores = [
        pltpu.make_async_copy(corrected_ref.at[t], corrected_hbm.at[t], out_sem.at[t])
        for t in range(tiles)
    ]
    for copy in stores:
        copy.start()
    for o in range(1, groups):
        source = lax.rem(g + groups - o, groups)
        pltpu.make_async_remote_copy(
            src_ref=outgoing.at[source], dst_ref=arrived.at[source],
            send_sem=cell_send.at[o], recv_sem=cell_recv.at[source],
            device_id=(source, d), device_id_type=MESH,
        ).wait_recv()
    there = [
        [home(positions_ref[(s * columns + d) * tiles + t]) for t in range(tiles)]
        for s in range(groups)
    ]
    slots = [
        pick((band == g, slot) for band, slot in there[s]) for s in range(groups)
    ]
    origin = [
        pick((slots[s] == j, s) for s in range(groups)) for j in range(tiles)
    ]
    for block in range(blocks):
        kind = 0 if block == 0 else 2 if block == blocks - 1 else 1
        total = None
        for row in range(ROWS):
            span = slice(row * COLS + block * BLOCK, row * COLS + (block + 1) * BLOCK)
            dark = dark_ref[:, span].astype(jnp.float32)
            inverse = inverse_ref[:, span]
            made = [
                ((arrived[origin[j], :, span].astype(jnp.float32) - dark) * inverse)
                .astype(jnp.bfloat16) for j in range(tiles)
            ]
            part = jnp.dot(
                jnp.concatenate(made, axis=0), weights[kind], preferred_element_type=jnp.float32
            )
            total = part if total is None else total + part
        lanes = slice(block * LANES, (block + 1) * LANES)
        total = total.astype(jnp.bfloat16).astype(jnp.float32)
        for j in range(tiles):
            placed[j, :, lanes] = total[j * planes:(j + 1) * planes]
    for j in range(tiles):
        cell = placed[j]
        base, shift = divmod(j * half_step, LANES)
        base = base * LANES
        if shift:
            cell = jnp.concatenate([cell, jnp.zeros((planes, LANES), jnp.float32)], axis=1)
            cell = pltpu.roll(cell, shift, 1)
        acc[:, base:base + cell.shape[1]] += cell

    @pl.when(d > 0)
    def _():
        spill = jnp.zeros((planes, LANES), jnp.float32)
        for o in range(groups):
            source = lax.rem(g + groups - o, groups)
            pltpu.make_async_remote_copy(
                src_ref=tail_out.at[source], dst_ref=tail_in.at[source],
                send_sem=tail_send.at[o], recv_sem=tail_recv.at[source],
                device_id=(source, lax.rem(d + columns - 1, columns)), device_id_type=MESH,
            ).wait_recv()
        before = [
            [home(positions_ref[(s * columns + d - 1) * tiles + t]) for t in range(tiles)]
            for s in range(groups)
        ]
        final = pick(
            ((band == g) & (slot == tiles - 1), s)
            for s in range(groups) for band, slot in before[s]
        )
        for row in range(ROWS):
            span = slice((row + 1) * COLS - OVL, (row + 1) * COLS)
            fixed = (
                (tail_in[final, row].astype(jnp.float32) - dark_ref[:, span].astype(jnp.float32))
                * inverse_ref[:, span]
            ).astype(jnp.bfloat16)
            spill = spill + jnp.dot(
                fixed, weights[2, BLOCK - OVL:, :], preferred_element_type=jnp.float32
            )
        spill = spill.astype(jnp.bfloat16).astype(jnp.float32)
        spill = pltpu.roll(spill, half_ovl, 1)
        lane = lax.broadcasted_iota(jnp.int32, (planes, LANES), 1)
        acc[:, 0:LANES] += jnp.where(lane < half_ovl, spill, 0.0)

    pooled_ref[...] = acc[:, 0:tiles * half_step].astype(jnp.bfloat16)
    for copy in sent:
        copy.wait_send()
    for copy in stores:
        copy.wait()
    for o in range(1, groups):
        cell_copy(o).wait_send()

    @pl.when(d < columns - 1)
    def _():
        for o in range(groups):
            tail_copy(o).wait_send()


def per_device(groups, columns, raw, dark, basis, counts, positions):
    tiles, planes, pixels = raw.shape
    half_step = (COLS - OVL) // 2
    bf16, f32 = jnp.bfloat16, jnp.float32
    vmem = pl.BlockSpec(memory_space=pltpu.VMEM)
    anywhere = pl.BlockSpec(memory_space=pl.ANY)
    dma = pltpu.SemaphoreType.DMA
    corrected, pooled = pl.pallas_call(
        functools.partial(kernel, groups, columns),
        out_shape=(
            jax.ShapeDtypeStruct(raw.shape, bf16),
            jax.ShapeDtypeStruct((planes, tiles * half_step), bf16),
        ),
        in_specs=[anywhere] * 5,
        out_specs=(anywhere, vmem),
        scratch_shapes=[
            pltpu.SMEM(counts.shape, jnp.int32),
            pltpu.SMEM(positions.shape, jnp.int32),
            pltpu.VMEM(raw.shape, bf16),
            pltpu.VMEM(dark.shape, bf16),
            pltpu.VMEM((16, pixels), bf16),
            pltpu.VMEM(raw.shape, bf16),
            pltpu.VMEM((planes, LANES), f32),
            pltpu.VMEM((groups, planes // 2, LANES), f32),
            pltpu.VMEM((columns, planes // 2, LANES), f32),
            pltpu.VMEM((3, BLOCK, LANES), bf16),
            pltpu.VMEM((groups, planes, pixels), bf16),
            pltpu.VMEM((groups, planes, pixels), bf16),
            pltpu.VMEM((groups, ROWS, planes, OVL), bf16),
            pltpu.VMEM((groups, ROWS, planes, OVL), bf16),
            pltpu.VMEM((planes, pixels), f32),
            pltpu.VMEM((tiles, planes, COLS // 2), f32),
            pltpu.VMEM((planes, tiles * half_step + LANES), f32),
            dma((4,)), dma((tiles,)), dma((tiles,)),
            dma((groups,)), dma((groups,)), dma((columns,)), dma((columns,)),
            dma((groups,)), dma((groups,)), dma((groups,)), dma((groups,)),
        ],
        compiler_params=pltpu.CompilerParams(
            collective_id=0, has_side_effects=True, vmem_limit_bytes=16 << 20
        ),
    )(*[pltpu.with_memory_space_constraint(x, pltpu.HBM) for x in (counts, positions, raw, dark, basis)])
    return corrected, pooled.reshape(1, planes, ROWS // 2, tiles * half_step)


def solution(mesh):
    in_specs = (P(("grp", "dev"), None, None), P(), P(), P(("grp", "dev")), P())
    out_specs = (P(("grp", "dev"), None, None), P("grp", None, None, "dev"))
    return jax.shard_map(
        functools.partial(per_device, mesh.shape["grp"], mesh.shape["dev"]),
        mesh=mesh, in_specs=in_specs, out_specs=out_specs, check_vma=False,
    )
```

```python
import functools

import jax
import jax.numpy as jnp
from jax import lax
from jax.experimental import pallas as pl
from jax.experimental.pallas import tpu as pltpu
from jax.sharding import PartitionSpec as P

ROWS = 2
COLS = 2048
OVL = 128
LANES = 128
BLOCK = 256
MESH = pl.DeviceIdType.MESH
NT = (((1,), (1,)), ((), ()))


def pick(options):
    found = jnp.int32(0)
    for hit, value in options:
        found = jnp.where(hit, value, found)
    return found


def pool_weights(block, blocks):
    row = lax.broadcasted_iota(jnp.int32, (BLOCK, LANES), 0)
    lane = lax.broadcasted_iota(jnp.int32, (BLOCK, LANES), 1)
    column = (row + block * BLOCK).astype(jnp.float32) + 0.5
    ramp = jnp.minimum(1.0, jnp.minimum(column / OVL, (blocks * BLOCK - column) / OVL))
    inside = (row >= 2 * lane) & (row < 2 * lane + 2)
    return jnp.where(inside, 0.25 * ramp, 0.0).astype(jnp.bfloat16)


def kernel(
    groups, columns,
    counts_hbm, positions_hbm, raw_hbm, dark_hbm, basis_hbm,
    corrected_hbm, pooled_ref,
    counts_ref, positions_ref, raw_ref, dark_ref, rhs, corrected_ref,
    stat, grp_buf, dev_buf, weights, outgoing, arrived, tail_out, tail_in, inverse_ref, placed, acc,
    in_sem, raw_sem, out_sem,
    grp_send, grp_recv, dev_send, dev_recv, cell_send, cell_recv, tail_send, tail_recv,
):
    tiles, planes, pixels = raw_ref.shape
    rank = basis_hbm.shape[0]
    band_size = columns * tiles
    half_step = (COLS - OVL) // 2
    half_ovl = OVL // 2
    blocks = COLS // BLOCK
    g = lax.axis_index("grp")
    d = lax.axis_index("dev")

    raw_loads = [
        pltpu.make_async_copy(raw_hbm.at[t], raw_ref.at[t], raw_sem.at[t]) for t in range(tiles)
    ]
    loads = [
        pltpu.make_async_copy(basis_hbm, rhs.at[0:rank], in_sem.at[0]),
        pltpu.make_async_copy(dark_hbm, dark_ref, in_sem.at[1]),
        pltpu.make_async_copy(counts_hbm, counts_ref, in_sem.at[2]),
        pltpu.make_async_copy(positions_hbm, positions_ref, in_sem.at[3]),
    ]
    for copy in loads[:2] + raw_loads + loads[2:]:
        copy.start()

    barrier = pltpu.get_barrier_semaphore()
    near = [lax.rem(d + 1, columns), lax.rem(d + columns - 1, columns)]
    for o in range(1, groups):
        other = lax.rem(g + o, groups)
        for where in [d] + near:
            pl.semaphore_signal(barrier, inc=1, device_id=(other, where), device_id_type=MESH)
    for o in range(1, columns):
        pl.semaphore_signal(
            barrier, inc=1, device_id=(g, lax.rem(d + o, columns)), device_id_type=MESH
        )

    rhs[rank:, :] = jnp.ones((rhs.shape[0] - rank, pixels), jnp.bfloat16)
    width = rhs.shape[0]
    weights[0] = pool_weights(0, blocks)
    weights[1] = pool_weights(1, blocks)
    weights[2] = pool_weights(blocks - 1, blocks)
    stat[...] = jnp.zeros_like(stat)
    for copy in loads:
        copy.wait()
    dark_sums = lax.dot_general(dark_ref[...], rhs[...], NT, preferred_element_type=jnp.float32)
    plane = lax.broadcasted_iota(jnp.int32, (planes, width), 0)
    for copy in raw_loads:
        copy.wait()
    sums = lax.dot_general(
        raw_ref[...].reshape(tiles * planes, pixels), rhs[...], NT,
        preferred_element_type=jnp.float32,
    )
    local = jnp.zeros((planes, width), jnp.float32)
    for t in range(tiles):
        part = sums[t * planes:(t + 1) * planes] - dark_sums
        local = local + jnp.where(plane < counts_ref[t], part, 0.0)
    stat[:, 0:width] = local
    half = planes // 2
    grp_buf[g] = stat[0:half, :] + pltpu.roll(stat[half:, :], LANES // 2, 1)

    def home(at):
        return lax.div(at, band_size), lax.rem(at, tiles)

    wide = lax.broadcasted_iota(jnp.int32, (planes, pixels), 0)
    mine = [home(positions_ref[(g * columns + d) * tiles + t]) for t in range(tiles)]
    for b in range(groups):
        chosen = pick((mine[t][0] == b, t) for t in range(tiles))
        masked = jnp.where(
            wide < counts_ref[chosen],
            raw_ref[chosen].astype(jnp.float32), dark_ref[...].astype(jnp.float32),
        ).astype(jnp.bfloat16)
        outgoing[b] = masked
        for row in range(ROWS):
            tail_out[b, row] = masked[:, (row + 1) * COLS - OVL:(row + 1) * COLS]
    arrived[g] = outgoing[g]

    pl.semaphore_wait(barrier, 3 * (groups - 1) + columns - 1)

    sent = []
    for o in range(1, groups):
        other = lax.rem(g + o, groups)
        copy = pltpu.make_async_remote_copy(
            src_ref=grp_buf.at[g], dst_ref=grp_buf.at[g],
            send_sem=grp_send.at[o], recv_sem=grp_recv.at[g],
            device_id=(other, d), device_id_type=MESH,
        )
        copy.start()
        sent.append(copy)

    def cell_copy(o):
        other = lax.rem(g + o, groups)
        return pltpu.make_async_remote_copy(
            src_ref=outgoing.at[other], dst_ref=arrived.at[g],
            send_sem=cell_send.at[o], recv_sem=cell_recv.at[g],
            device_id=(other, d), device_id_type=MESH,
        )

    def tail_copy(o):
        other = lax.rem(g + o, groups)
        return pltpu.make_async_remote_copy(
            src_ref=tail_out.at[other], dst_ref=tail_in.at[g],
            send_sem=tail_send.at[o], recv_sem=tail_recv.at[g],
            device_id=(other, lax.rem(d + 1, columns)), device_id_type=MESH,
        )

    @pl.when(d < columns - 1)
    def _():
        for o in range(groups):
            tail_copy(o).start()

    for o in range(1, groups):
        cell_copy(o).start()

    for o in range(1, groups):
        source = lax.rem(g + groups - o, groups)
        pltpu.make_async_remote_copy(
            src_ref=grp_buf.at[source], dst_ref=grp_buf.at[source],
            send_sem=grp_send.at[o], recv_sem=grp_recv.at[source],
            device_id=(source, d), device_id_type=MESH,
        ).wait_recv()
    dev_buf[d] = jnp.sum(grp_buf[...], axis=0)
    for o in range(1, columns):
        copy = pltpu.make_async_remote_copy(
            src_ref=dev_buf.at[d], dst_ref=dev_buf.at[d],
            send_sem=dev_send.at[o], recv_sem=dev_recv.at[d],
            device_id=(g, lax.rem(d + o, columns)), device_id_type=MESH,
        )
        copy.start()
        sent.append(copy)
    acc[...] = jnp.zeros_like(acc)
    for o in range(1, columns):
        source = lax.rem(d + columns - o, columns)
        pltpu.make_async_remote_copy(
            src_ref=dev_buf.at[source], dst_ref=dev_buf.at[source],
            send_sem=dev_send.at[o], recv_sem=dev_recv.at[source],
            device_id=(g, source), device_id_type=MESH,
        ).wait_recv()
    packed = jnp.sum(dev_buf[...], axis=0)
    full = jnp.concatenate([packed, pltpu.roll(packed, LANES // 2, 1)], axis=0)
    coef = full[:, 0:rank] / full[:, rank:rank + 1]
    high = coef.astype(jnp.bfloat16)
    rest = coef - high.astype(jnp.float32)
    middle = rest.astype(jnp.bfloat16)
    low = (rest - middle.astype(jnp.float32)).astype(jnp.bfloat16)

    parts = jnp.concatenate([low, middle, high], axis=1)
    plane = lax.broadcasted_iota(jnp.int32, (planes, BLOCK), 0)
    live = [plane < counts_ref[t] for t in range(tiles)]
    for block in range(pixels // BLOCK):
        span = slice(block * BLOCK, (block + 1) * BLOCK)
        basis = rhs[0:rank, span]
        shade = jnp.dot(
            parts, jnp.concatenate([basis, basis, basis], axis=0),
            preferred_element_type=jnp.float32,
        )
        inverse = jnp.exp(-shade)
        inverse_ref[:, span] = inverse
        dark = dark_ref[:, span].astype(jnp.float32)
        for t in range(tiles):
            fixed = (raw_ref[t, :, span].astype(jnp.float32) - dark) * inverse
            corrected_ref[t, :, span] = jnp.where(live[t], fixed, 0.0).astype(jnp.bfloat16)

    stores = [
        pltpu.make_async_copy(corrected_ref.at[t], corrected_hbm.at[t], out_sem.at[t])
        for t in range(tiles)
    ]
    for copy in stores:
        copy.start()
    for o in range(1, groups):
        source = lax.rem(g + groups - o, groups)
        pltpu.make_async_remote_copy(
            src_ref=outgoing.at[source], dst_ref=arrived.at[source],
            send_sem=cell_send.at[o], recv_sem=cell_recv.at[source],
            device_id=(source, d), device_id_type=MESH,
        ).wait_recv()
    there = [
        [home(positions_ref[(s * columns + d) * tiles + t]) for t in range(tiles)]
        for s in range(groups)
    ]
    slots = [
        pick((band == g, slot) for band, slot in there[s]) for s in range(groups)
    ]
    origin = [
        pick((slots[s] == j, s) for s in range(groups)) for j in range(tiles)
    ]
    for block in range(blocks):
        kind = 0 if block == 0 else 2 if block == blocks - 1 else 1
        total = None
        for row in range(ROWS):
            span = slice(row * COLS + block * BLOCK, row * COLS + (block + 1) * BLOCK)
            dark = dark_ref[:, span].astype(jnp.float32)
            inverse = inverse_ref[:, span]
            made = [
                ((arrived[origin[j], :, span].astype(jnp.float32) - dark) * inverse)
                .astype(jnp.bfloat16) for j in range(tiles)
            ]
            part = jnp.dot(
                jnp.concatenate(made, axis=0), weights[kind], preferred_element_type=jnp.float32
            )
            total = part if total is None else total + part
        lanes = slice(block * LANES, (block + 1) * LANES)
        total = total.astype(jnp.bfloat16).astype(jnp.float32)
        for j in range(tiles):
            placed[j, :, lanes] = total[j * planes:(j + 1) * planes]
    for j in range(tiles):
        cell = placed[j]
        base, shift = divmod(j * half_step, LANES)
        base = base * LANES
        if shift:
            cell = jnp.concatenate([cell, jnp.zeros((planes, LANES), jnp.float32)], axis=1)
            cell = pltpu.roll(cell, shift, 1)
        acc[:, base:base + cell.shape[1]] += cell

    @pl.when(d > 0)
    def _():
        spill = jnp.zeros((planes, LANES), jnp.float32)
        for o in range(groups):
            source = lax.rem(g + groups - o, groups)
            pltpu.make_async_remote_copy(
                src_ref=tail_out.at[source], dst_ref=tail_in.at[source],
                send_sem=tail_send.at[o], recv_sem=tail_recv.at[source],
                device_id=(source, lax.rem(d + columns - 1, columns)), device_id_type=MESH,
            ).wait_recv()
        before = [
            [home(positions_ref[(s * columns + d - 1) * tiles + t]) for t in range(tiles)]
            for s in range(groups)
        ]
        final = pick(
            ((band == g) & (slot == tiles - 1), s)
            for s in range(groups) for band, slot in before[s]
        )
        for row in range(ROWS):
            span = slice((row + 1) * COLS - OVL, (row + 1) * COLS)
            fixed = (
                (tail_in[final, row].astype(jnp.float32) - dark_ref[:, span].astype(jnp.float32))
                * inverse_ref[:, span]
            ).astype(jnp.bfloat16)
            spill = spill + jnp.dot(
                fixed, weights[2, BLOCK - OVL:, :], preferred_element_type=jnp.float32
            )
        spill = spill.astype(jnp.bfloat16).astype(jnp.float32)
        spill = pltpu.roll(spill, half_ovl, 1)
        lane = lax.broadcasted_iota(jnp.int32, (planes, LANES), 1)
        acc[:, 0:LANES] += jnp.where(lane < half_ovl, spill, 0.0)

    pooled_ref[...] = acc[:, 0:tiles * half_step].astype(jnp.bfloat16)
    for copy in sent:
        copy.wait_send()
    for copy in stores:
        copy.wait()
    for o in range(1, groups):
        cell_copy(o).wait_send()

    @pl.when(d < columns - 1)
    def _():
        for o in range(groups):
            tail_copy(o).wait_send()


def deliver(corrected_ref, pooled_ref, corrected_out, pooled_out, sems):
    tiles = corrected_ref.shape[0]
    copies = [pltpu.make_async_copy(pooled_ref, pooled_out, sems.at[tiles])]
    for t in range(tiles):
        copies.append(pltpu.make_async_copy(corrected_ref.at[t], corrected_out.at[t], sems.at[t]))
    for copy in copies:
        copy.start()
    for copy in copies:
        copy.wait()


def per_device(groups, columns, raw, dark, basis, counts, positions):
    tiles, planes, pixels = raw.shape
    half_step = (COLS - OVL) // 2
    bf16, f32 = jnp.bfloat16, jnp.float32
    vmem = pl.BlockSpec(memory_space=pltpu.VMEM)
    anywhere = pl.BlockSpec(memory_space=pl.ANY)
    dma = pltpu.SemaphoreType.DMA
    corrected, pooled = pl.pallas_call(
        functools.partial(kernel, groups, columns),
        out_shape=(
            jax.ShapeDtypeStruct(raw.shape, bf16),
            jax.ShapeDtypeStruct((planes, tiles * half_step), bf16),
        ),
        in_specs=[anywhere] * 5,
        out_specs=(anywhere, vmem),
        scratch_shapes=[
            pltpu.SMEM(counts.shape, jnp.int32),
            pltpu.SMEM(positions.shape, jnp.int32),
            pltpu.VMEM(raw.shape, bf16),
            pltpu.VMEM(dark.shape, bf16),
            pltpu.VMEM((16, pixels), bf16),
            pltpu.VMEM(raw.shape, bf16),
            pltpu.VMEM((planes, LANES), f32),
            pltpu.VMEM((groups, planes // 2, LANES), f32),
            pltpu.VMEM((columns, planes // 2, LANES), f32),
            pltpu.VMEM((3, BLOCK, LANES), bf16),
            pltpu.VMEM((groups, planes, pixels), bf16),
            pltpu.VMEM((groups, planes, pixels), bf16),
            pltpu.VMEM((groups, ROWS, planes, OVL), bf16),
            pltpu.VMEM((groups, ROWS, planes, OVL), bf16),
            pltpu.VMEM((planes, pixels), f32),
            pltpu.VMEM((tiles, planes, COLS // 2), f32),
            pltpu.VMEM((planes, tiles * half_step + LANES), f32),
            dma((4,)), dma((tiles,)), dma((tiles,)),
            dma((groups,)), dma((groups,)), dma((columns,)), dma((columns,)),
            dma((groups,)), dma((groups,)), dma((groups,)), dma((groups,)),
        ],
        compiler_params=pltpu.CompilerParams(
            collective_id=0, has_side_effects=True, vmem_limit_bytes=16 << 20
        ),
    )(*[pltpu.with_memory_space_constraint(x, pltpu.HBM) for x in (counts, positions, raw, dark, basis)])
    corrected, pooled = pl.pallas_call(
        deliver,
        out_shape=(
            jax.ShapeDtypeStruct(corrected.shape, bf16),
            jax.ShapeDtypeStruct(pooled.shape, bf16),
        ),
        in_specs=[anywhere] * 2,
        out_specs=(anywhere, anywhere),
        scratch_shapes=[dma((tiles + 1,))],
        compiler_params=pltpu.CompilerParams(vmem_limit_bytes=1 << 20),
    )(corrected, pooled)
    return corrected, pooled.reshape(1, planes, ROWS // 2, tiles * half_step)


def solution(mesh):
    in_specs = (P(("grp", "dev"), None, None), P(), P(), P(("grp", "dev")), P())
    out_specs = (P(("grp", "dev"), None, None), P("grp", None, None, "dev"))
    return jax.shard_map(
        functools.partial(per_device, mesh.shape["grp"], mesh.shape["dev"]),
        mesh=mesh, in_specs=in_specs, out_specs=out_specs, check_vma=False,
    )
```

```python
import functools

import jax
import jax.numpy as jnp
from jax import lax
from jax.experimental import pallas as pl
from jax.experimental.pallas import tpu as pltpu
from jax.sharding import PartitionSpec as P

ROWS = 2
COLS = 2048
OVL = 128
LANES = 128
BLOCK = 256
MESH = pl.DeviceIdType.MESH
NT = (((1,), (1,)), ((), ()))


def pick(options):
    found = jnp.int32(0)
    for hit, value in options:
        found = jnp.where(hit, value, found)
    return found


def pool_weights(block, blocks):
    row = lax.broadcasted_iota(jnp.int32, (BLOCK, LANES), 0)
    lane = lax.broadcasted_iota(jnp.int32, (BLOCK, LANES), 1)
    column = (row + block * BLOCK).astype(jnp.float32) + 0.5
    ramp = jnp.minimum(1.0, jnp.minimum(column / OVL, (blocks * BLOCK - column) / OVL))
    inside = (row >= 2 * lane) & (row < 2 * lane + 2)
    return jnp.where(inside, 0.25 * ramp, 0.0).astype(jnp.bfloat16)


def kernel(
    groups, columns,
    counts_hbm, positions_hbm, raw_hbm, dark_hbm, basis_hbm,
    corrected_hbm, pooled_ref,
    counts_ref, positions_ref, raw_ref, dark_ref, rhs, corrected_ref,
    stat, grp_buf, dev_buf, weights, outgoing, arrived, tail_out, tail_in, inverse_ref, placed, acc,
    in_sem, raw_sem, out_sem,
    grp_send, grp_recv, dev_send, dev_recv, cell_send, cell_recv, tail_send, tail_recv,
):
    tiles, planes, pixels = raw_ref.shape
    rank = basis_hbm.shape[0]
    band_size = columns * tiles
    half_step = (COLS - OVL) // 2
    half_ovl = OVL // 2
    blocks = COLS // BLOCK
    g = lax.axis_index("grp")
    d = lax.axis_index("dev")

    raw_loads = [pltpu.make_async_copy(raw_hbm, raw_ref, raw_sem.at[0])]
    loads = [
        pltpu.make_async_copy(basis_hbm, rhs.at[0:rank], in_sem.at[0]),
        pltpu.make_async_copy(dark_hbm, dark_ref, in_sem.at[1]),
        pltpu.make_async_copy(counts_hbm, counts_ref, in_sem.at[2]),
        pltpu.make_async_copy(positions_hbm, positions_ref, in_sem.at[3]),
    ]
    for copy in loads[:2] + raw_loads + loads[2:]:
        copy.start()

    barrier = pltpu.get_barrier_semaphore()
    near = [lax.rem(d + 1, columns), lax.rem(d + columns - 1, columns)]
    for o in range(1, groups):
        other = lax.rem(g + o, groups)
        for where in [d] + near:
            pl.semaphore_signal(barrier, inc=1, device_id=(other, where), device_id_type=MESH)
    for o in range(1, columns):
        pl.semaphore_signal(
            barrier, inc=1, device_id=(g, lax.rem(d + o, columns)), device_id_type=MESH
        )

    rhs[rank:, :] = jnp.ones((rhs.shape[0] - rank, pixels), jnp.bfloat16)
    width = rhs.shape[0]
    weights[0] = pool_weights(0, blocks)
    weights[1] = pool_weights(1, blocks)
    weights[2] = pool_weights(blocks - 1, blocks)
    stat[...] = jnp.zeros_like(stat)
    for copy in loads:
        copy.wait()
    dark_sums = lax.dot_general(dark_ref[...], rhs[...], NT, preferred_element_type=jnp.float32)
    plane = lax.broadcasted_iota(jnp.int32, (planes, width), 0)
    for copy in raw_loads:
        copy.wait()
    sums = lax.dot_general(
        raw_ref[...].reshape(tiles * planes, pixels), rhs[...], NT,
        preferred_element_type=jnp.float32,
    )
    local = jnp.zeros((planes, width), jnp.float32)
    for t in range(tiles):
        part = sums[t * planes:(t + 1) * planes] - dark_sums
        local = local + jnp.where(plane < counts_ref[t], part, 0.0)
    stat[:, 0:width] = local
    half = planes // 2
    grp_buf[g] = stat[0:half, :] + pltpu.roll(stat[half:, :], LANES // 2, 1)

    pl.semaphore_wait(barrier, 3 * (groups - 1) + columns - 1)

    sent = []
    for o in range(1, groups):
        other = lax.rem(g + o, groups)
        copy = pltpu.make_async_remote_copy(
            src_ref=grp_buf.at[g], dst_ref=grp_buf.at[g],
            send_sem=grp_send.at[o], recv_sem=grp_recv.at[g],
            device_id=(other, d), device_id_type=MESH,
        )
        copy.start()
        sent.append(copy)

    def home(at):
        return lax.div(at, band_size), lax.rem(at, tiles)

    wide = lax.broadcasted_iota(jnp.int32, (planes, pixels), 0)
    mine = [home(positions_ref[(g * columns + d) * tiles + t]) for t in range(tiles)]
    for b in range(groups):
        chosen = pick((mine[t][0] == b, t) for t in range(tiles))
        masked = jnp.where(
            wide < counts_ref[chosen],
            raw_ref[chosen].astype(jnp.float32), dark_ref[...].astype(jnp.float32),
        ).astype(jnp.bfloat16)
        outgoing[b] = masked
        for row in range(ROWS):
            tail_out[b, row] = masked[:, (row + 1) * COLS - OVL:(row + 1) * COLS]
    arrived[g] = outgoing[g]

    def cell_copy(o):
        other = lax.rem(g + o, groups)
        return pltpu.make_async_remote_copy(
            src_ref=outgoing.at[other], dst_ref=arrived.at[g],
            send_sem=cell_send.at[o], recv_sem=cell_recv.at[g],
            device_id=(other, d), device_id_type=MESH,
        )

    def tail_copy(o):
        other = lax.rem(g + o, groups)
        return pltpu.make_async_remote_copy(
            src_ref=tail_out.at[other], dst_ref=tail_in.at[g],
            send_sem=tail_send.at[o], recv_sem=tail_recv.at[g],
            device_id=(other, lax.rem(d + 1, columns)), device_id_type=MESH,
        )

    @pl.when(d < columns - 1)
    def _():
        for o in range(groups):
            tail_copy(o).start()

    for o in range(1, groups):
        cell_copy(o).start()

    for o in range(1, groups):
        source = lax.rem(g + groups - o, groups)
        pltpu.make_async_remote_copy(
            src_ref=grp_buf.at[source], dst_ref=grp_buf.at[source],
            send_sem=grp_send.at[o], recv_sem=grp_recv.at[source],
            device_id=(source, d), device_id_type=MESH,
        ).wait_recv()
    dev_buf[d] = jnp.sum(grp_buf[...], axis=0)
    for o in range(1, columns):
        copy = pltpu.make_async_remote_copy(
            src_ref=dev_buf.at[d], dst_ref=dev_buf.at[d],
            send_sem=dev_send.at[o], recv_sem=dev_recv.at[d],
            device_id=(g, lax.rem(d + o, columns)), device_id_type=MESH,
        )
        copy.start()
        sent.append(copy)
    acc[...] = jnp.zeros_like(acc)
    for o in range(1, columns):
        source = lax.rem(d + columns - o, columns)
        pltpu.make_async_remote_copy(
            src_ref=dev_buf.at[source], dst_ref=dev_buf.at[source],
            send_sem=dev_send.at[o], recv_sem=dev_recv.at[source],
            device_id=(g, source), device_id_type=MESH,
        ).wait_recv()
    packed = jnp.sum(dev_buf[...], axis=0)
    full = jnp.concatenate([packed, pltpu.roll(packed, LANES // 2, 1)], axis=0)
    coef = full[:, 0:rank] / full[:, rank:rank + 1]
    high = coef.astype(jnp.bfloat16)
    rest = coef - high.astype(jnp.float32)
    middle = rest.astype(jnp.bfloat16)
    low = (rest - middle.astype(jnp.float32)).astype(jnp.bfloat16)

    parts = jnp.concatenate([low, middle, high], axis=1)
    plane = lax.broadcasted_iota(jnp.int32, (planes, BLOCK), 0)
    live = [plane < counts_ref[t] for t in range(tiles)]
    for block in range(pixels // BLOCK):
        span = slice(block * BLOCK, (block + 1) * BLOCK)
        basis = rhs[0:rank, span]
        shade = jnp.dot(
            parts, jnp.concatenate([basis, basis, basis], axis=0),
            preferred_element_type=jnp.float32,
        )
        inverse = jnp.exp(-shade)
        inverse_ref[:, span] = inverse
        dark = dark_ref[:, span].astype(jnp.float32)
        for t in range(tiles):
            fixed = (raw_ref[t, :, span].astype(jnp.float32) - dark) * inverse
            corrected_ref[t, :, span] = jnp.where(live[t], fixed, 0.0).astype(jnp.bfloat16)

    stores = [pltpu.make_async_copy(corrected_ref, corrected_hbm, out_sem.at[0])]
    for copy in stores:
        copy.start()
    for o in range(1, groups):
        source = lax.rem(g + groups - o, groups)
        pltpu.make_async_remote_copy(
            src_ref=outgoing.at[source], dst_ref=arrived.at[source],
            send_sem=cell_send.at[o], recv_sem=cell_recv.at[source],
            device_id=(source, d), device_id_type=MESH,
        ).wait_recv()
    there = [
        [home(positions_ref[(s * columns + d) * tiles + t]) for t in range(tiles)]
        for s in range(groups)
    ]
    slots = [
        pick((band == g, slot) for band, slot in there[s]) for s in range(groups)
    ]
    origin = [
        pick((slots[s] == j, s) for s in range(groups)) for j in range(tiles)
    ]
    for block in range(blocks):
        kind = 0 if block == 0 else 2 if block == blocks - 1 else 1
        total = None
        for row in range(ROWS):
            span = slice(row * COLS + block * BLOCK, row * COLS + (block + 1) * BLOCK)
            dark = dark_ref[:, span].astype(jnp.float32)
            inverse = inverse_ref[:, span]
            made = [
                ((arrived[origin[j], :, span].astype(jnp.float32) - dark) * inverse)
                .astype(jnp.bfloat16) for j in range(tiles)
            ]
            part = jnp.dot(
                jnp.concatenate(made, axis=0), weights[kind], preferred_element_type=jnp.float32
            )
            total = part if total is None else total + part
        lanes = slice(block * LANES, (block + 1) * LANES)
        total = total.astype(jnp.bfloat16).astype(jnp.float32)
        for j in range(tiles):
            placed[j, :, lanes] = total[j * planes:(j + 1) * planes]
    for j in range(tiles):
        cell = placed[j]
        base, shift = divmod(j * half_step, LANES)
        base = base * LANES
        if shift:
            cell = jnp.concatenate([cell, jnp.zeros((planes, LANES), jnp.float32)], axis=1)
            cell = pltpu.roll(cell, shift, 1)
        acc[:, base:base + cell.shape[1]] += cell

    @pl.when(d > 0)
    def _():
        spill = jnp.zeros((planes, LANES), jnp.float32)
        for o in range(groups):
            source = lax.rem(g + groups - o, groups)
            pltpu.make_async_remote_copy(
                src_ref=tail_out.at[source], dst_ref=tail_in.at[source],
                send_sem=tail_send.at[o], recv_sem=tail_recv.at[source],
                device_id=(source, lax.rem(d + columns - 1, columns)), device_id_type=MESH,
            ).wait_recv()
        before = [
            [home(positions_ref[(s * columns + d - 1) * tiles + t]) for t in range(tiles)]
            for s in range(groups)
        ]
        final = pick(
            ((band == g) & (slot == tiles - 1), s)
            for s in range(groups) for band, slot in before[s]
        )
        for row in range(ROWS):
            span = slice((row + 1) * COLS - OVL, (row + 1) * COLS)
            fixed = (
                (tail_in[final, row].astype(jnp.float32) - dark_ref[:, span].astype(jnp.float32))
                * inverse_ref[:, span]
            ).astype(jnp.bfloat16)
            spill = spill + jnp.dot(
                fixed, weights[2, BLOCK - OVL:, :], preferred_element_type=jnp.float32
            )
        spill = spill.astype(jnp.bfloat16).astype(jnp.float32)
        spill = pltpu.roll(spill, half_ovl, 1)
        lane = lax.broadcasted_iota(jnp.int32, (planes, LANES), 1)
        acc[:, 0:LANES] += jnp.where(lane < half_ovl, spill, 0.0)

    pooled_ref[...] = acc[:, 0:tiles * half_step].astype(jnp.bfloat16)
    for copy in sent:
        copy.wait_send()
    for copy in stores:
        copy.wait()
    for o in range(1, groups):
        cell_copy(o).wait_send()

    @pl.when(d < columns - 1)
    def _():
        for o in range(groups):
            tail_copy(o).wait_send()


def deliver(corrected_ref, pooled_ref, corrected_out, pooled_out, sems):
    tiles = corrected_ref.shape[0]
    copies = [pltpu.make_async_copy(pooled_ref, pooled_out, sems.at[tiles])]
    for t in range(tiles):
        copies.append(pltpu.make_async_copy(corrected_ref.at[t], corrected_out.at[t], sems.at[t]))
    for copy in copies:
        copy.start()
    for copy in copies:
        copy.wait()


def per_device(groups, columns, raw, dark, basis, counts, positions):
    tiles, planes, pixels = raw.shape
    half_step = (COLS - OVL) // 2
    bf16, f32 = jnp.bfloat16, jnp.float32
    vmem = pl.BlockSpec(memory_space=pltpu.VMEM)
    anywhere = pl.BlockSpec(memory_space=pl.ANY)
    dma = pltpu.SemaphoreType.DMA
    corrected, pooled = pl.pallas_call(
        functools.partial(kernel, groups, columns),
        out_shape=(
            jax.ShapeDtypeStruct(raw.shape, bf16),
            jax.ShapeDtypeStruct((planes, tiles * half_step), bf16),
        ),
        in_specs=[anywhere] * 5,
        out_specs=(anywhere, vmem),
        scratch_shapes=[
            pltpu.SMEM(counts.shape, jnp.int32),
            pltpu.SMEM(positions.shape, jnp.int32),
            pltpu.VMEM(raw.shape, bf16),
            pltpu.VMEM(dark.shape, bf16),
            pltpu.VMEM((16, pixels), bf16),
            pltpu.VMEM(raw.shape, bf16),
            pltpu.VMEM((planes, LANES), f32),
            pltpu.VMEM((groups, planes // 2, LANES), f32),
            pltpu.VMEM((columns, planes // 2, LANES), f32),
            pltpu.VMEM((3, BLOCK, LANES), bf16),
            pltpu.VMEM((groups, planes, pixels), bf16),
            pltpu.VMEM((groups, planes, pixels), bf16),
            pltpu.VMEM((groups, ROWS, planes, OVL), bf16),
            pltpu.VMEM((groups, ROWS, planes, OVL), bf16),
            pltpu.VMEM((planes, pixels), f32),
            pltpu.VMEM((tiles, planes, COLS // 2), f32),
            pltpu.VMEM((planes, tiles * half_step + LANES), f32),
            dma((4,)), dma((1,)), dma((1,)),
            dma((groups,)), dma((groups,)), dma((columns,)), dma((columns,)),
            dma((groups,)), dma((groups,)), dma((groups,)), dma((groups,)),
        ],
        compiler_params=pltpu.CompilerParams(
            collective_id=0, has_side_effects=True, vmem_limit_bytes=16 << 20
        ),
    )(*[pltpu.with_memory_space_constraint(x, pltpu.HBM) for x in (counts, positions, raw, dark, basis)])
    corrected, pooled = pl.pallas_call(
        deliver,
        out_shape=(
            jax.ShapeDtypeStruct(corrected.shape, bf16),
            jax.ShapeDtypeStruct(pooled.shape, bf16),
        ),
        in_specs=[anywhere] * 2,
        out_specs=(anywhere, anywhere),
        scratch_shapes=[dma((tiles + 1,))],
        compiler_params=pltpu.CompilerParams(vmem_limit_bytes=1 << 20),
    )(corrected, pooled)
    return corrected, pooled.reshape(1, planes, ROWS // 2, tiles * half_step)


def solution(mesh):
    in_specs = (P(("grp", "dev"), None, None), P(), P(), P(("grp", "dev")), P())
    out_specs = (P(("grp", "dev"), None, None), P("grp", None, None, "dev"))
    return jax.shard_map(
        functools.partial(per_device, mesh.shape["grp"], mesh.shape["dev"]),
        mesh=mesh, in_specs=in_specs, out_specs=out_specs, check_vma=False,
    )
```

```python
import functools

import jax
import jax.numpy as jnp
from jax import lax
from jax.experimental import pallas as pl
from jax.experimental.pallas import tpu as pltpu
from jax.sharding import PartitionSpec as P

ROWS = 2
COLS = 2048
OVL = 128
LANES = 128
BLOCK = 256
MESH = pl.DeviceIdType.MESH
NT = (((1,), (1,)), ((), ()))


def pick(options):
    found = jnp.int32(0)
    for hit, value in options:
        found = jnp.where(hit, value, found)
    return found


def pool_weights(block, blocks):
    row = lax.broadcasted_iota(jnp.int32, (BLOCK, LANES), 0)
    lane = lax.broadcasted_iota(jnp.int32, (BLOCK, LANES), 1)
    column = (row + block * BLOCK).astype(jnp.float32) + 0.5
    ramp = jnp.minimum(1.0, jnp.minimum(column / OVL, (blocks * BLOCK - column) / OVL))
    inside = (row >= 2 * lane) & (row < 2 * lane + 2)
    return jnp.where(inside, 0.25 * ramp, 0.0).astype(jnp.bfloat16)


def kernel(
    groups, columns,
    counts_hbm, positions_hbm, raw_hbm, dark_hbm, basis_hbm,
    corrected_hbm, pooled_ref,
    counts_ref, positions_ref, raw_ref, dark_ref, rhs, corrected_ref,
    stat, grp_buf, dev_buf, weights, outgoing, arrived, tail_out, tail_in, inverse_ref, placed, acc, diff, stack,
    in_sem, raw_sem, out_sem,
    grp_send, grp_recv, dev_send, dev_recv, cell_send, cell_recv, tail_send, tail_recv,
):
    tiles, planes, pixels = raw_ref.shape
    rank = basis_hbm.shape[0]
    band_size = columns * tiles
    half_step = (COLS - OVL) // 2
    half_ovl = OVL // 2
    blocks = COLS // BLOCK
    g = lax.axis_index("grp")
    d = lax.axis_index("dev")

    raw_loads = [pltpu.make_async_copy(raw_hbm, raw_ref, raw_sem.at[0])]
    loads = [
        pltpu.make_async_copy(basis_hbm, rhs.at[0:rank], in_sem.at[0]),
        pltpu.make_async_copy(dark_hbm, dark_ref, in_sem.at[1]),
        pltpu.make_async_copy(counts_hbm, counts_ref, in_sem.at[2]),
        pltpu.make_async_copy(positions_hbm, positions_ref, in_sem.at[3]),
    ]
    for copy in loads[:2] + raw_loads + loads[2:]:
        copy.start()

    barrier = pltpu.get_barrier_semaphore()
    near = [lax.rem(d + 1, columns), lax.rem(d + columns - 1, columns)]
    for o in range(1, groups):
        other = lax.rem(g + o, groups)
        for where in [d] + near:
            pl.semaphore_signal(barrier, inc=1, device_id=(other, where), device_id_type=MESH)
    for o in range(1, columns):
        pl.semaphore_signal(
            barrier, inc=1, device_id=(g, lax.rem(d + o, columns)), device_id_type=MESH
        )

    rhs[rank:, :] = jnp.ones((rhs.shape[0] - rank, pixels), jnp.bfloat16)
    width = rhs.shape[0]
    weights[0] = pool_weights(0, blocks)
    weights[1] = pool_weights(1, blocks)
    weights[2] = pool_weights(blocks - 1, blocks)
    stat[...] = jnp.zeros_like(stat)
    for copy in loads:
        copy.wait()
    dark_sums = lax.dot_general(dark_ref[...], rhs[...], NT, preferred_element_type=jnp.float32)
    plane = lax.broadcasted_iota(jnp.int32, (planes, width), 0)
    for copy in raw_loads:
        copy.wait()
    sums = lax.dot_general(
        raw_ref[...].reshape(tiles * planes, pixels), rhs[...], NT,
        preferred_element_type=jnp.float32,
    )
    local = jnp.zeros((planes, width), jnp.float32)
    for t in range(tiles):
        part = sums[t * planes:(t + 1) * planes] - dark_sums
        local = local + jnp.where(plane < counts_ref[t], part, 0.0)
    stat[:, 0:width] = local
    half = planes // 2
    grp_buf[g] = stat[0:half, :] + pltpu.roll(stat[half:, :], LANES // 2, 1)

    pl.semaphore_wait(barrier, 3 * (groups - 1) + columns - 1)

    sent = []
    for o in range(1, groups):
        other = lax.rem(g + o, groups)
        copy = pltpu.make_async_remote_copy(
            src_ref=grp_buf.at[g], dst_ref=grp_buf.at[g],
            send_sem=grp_send.at[o], recv_sem=grp_recv.at[g],
            device_id=(other, d), device_id_type=MESH,
        )
        copy.start()
        sent.append(copy)

    def home(at):
        return lax.div(at, band_size), lax.rem(at, tiles)

    wide = lax.broadcasted_iota(jnp.int32, (planes, pixels), 0)
    mine = [home(positions_ref[(g * columns + d) * tiles + t]) for t in range(tiles)]
    for b in range(groups):
        chosen = pick((mine[t][0] == b, t) for t in range(tiles))
        masked = jnp.where(
            wide < counts_ref[chosen],
            raw_ref[chosen].astype(jnp.float32), dark_ref[...].astype(jnp.float32),
        ).astype(jnp.bfloat16)
        outgoing[b] = masked
        for row in range(ROWS):
            tail_out[b, row] = masked[:, (row + 1) * COLS - OVL:(row + 1) * COLS]
    arrived[g] = outgoing[g]

    def cell_copy(o):
        other = lax.rem(g + o, groups)
        return pltpu.make_async_remote_copy(
            src_ref=outgoing.at[other], dst_ref=arrived.at[g],
            send_sem=cell_send.at[o], recv_sem=cell_recv.at[g],
            device_id=(other, d), device_id_type=MESH,
        )

    def tail_copy(o):
        other = lax.rem(g + o, groups)
        return pltpu.make_async_remote_copy(
            src_ref=tail_out.at[other], dst_ref=tail_in.at[g],
            send_sem=tail_send.at[o], recv_sem=tail_recv.at[g],
            device_id=(other, lax.rem(d + 1, columns)), device_id_type=MESH,
        )

    @pl.when(d < columns - 1)
    def _():
        for o in range(groups):
            tail_copy(o).start()

    for o in range(1, groups):
        cell_copy(o).start()

    for i in range(3):
        stack[i * rank:(i + 1) * rank, :] = rhs[0:rank, :]
    for t in range(tiles):
        bare = raw_ref[t].astype(jnp.float32) - dark_ref[...].astype(jnp.float32)
        diff[t] = jnp.where(wide < counts_ref[t], bare, 0.0)
    for o in range(1, groups):
        source = lax.rem(g + groups - o, groups)
        pltpu.make_async_remote_copy(
            src_ref=grp_buf.at[source], dst_ref=grp_buf.at[source],
            send_sem=grp_send.at[o], recv_sem=grp_recv.at[source],
            device_id=(source, d), device_id_type=MESH,
        ).wait_recv()
    dev_buf[d] = jnp.sum(grp_buf[...], axis=0)
    for o in range(1, columns):
        copy = pltpu.make_async_remote_copy(
            src_ref=dev_buf.at[d], dst_ref=dev_buf.at[d],
            send_sem=dev_send.at[o], recv_sem=dev_recv.at[d],
            device_id=(g, lax.rem(d + o, columns)), device_id_type=MESH,
        )
        copy.start()
        sent.append(copy)
    acc[...] = jnp.zeros_like(acc)
    for o in range(1, columns):
        source = lax.rem(d + columns - o, columns)
        pltpu.make_async_remote_copy(
            src_ref=dev_buf.at[source], dst_ref=dev_buf.at[source],
            send_sem=dev_send.at[o], recv_sem=dev_recv.at[source],
            device_id=(g, source), device_id_type=MESH,
        ).wait_recv()
    packed = jnp.sum(dev_buf[...], axis=0)
    full = jnp.concatenate([packed, pltpu.roll(packed, LANES // 2, 1)], axis=0)
    coef = full[:, 0:rank] / full[:, rank:rank + 1]
    high = coef.astype(jnp.bfloat16)
    rest = coef - high.astype(jnp.float32)
    middle = rest.astype(jnp.bfloat16)
    low = (rest - middle.astype(jnp.float32)).astype(jnp.bfloat16)

    parts = jnp.concatenate([low, middle, high], axis=1)
    for block in range(pixels // BLOCK):
        span = slice(block * BLOCK, (block + 1) * BLOCK)
        shade = jnp.dot(parts, stack[:, span], preferred_element_type=jnp.float32)
        inverse = jnp.exp(-shade)
        inverse_ref[:, span] = inverse
        for t in range(tiles):
            corrected_ref[t, :, span] = (diff[t, :, span] * inverse).astype(jnp.bfloat16)

    stores = [pltpu.make_async_copy(corrected_ref, corrected_hbm, out_sem.at[0])]
    for copy in stores:
        copy.start()
    for o in range(1, groups):
        source = lax.rem(g + groups - o, groups)
        pltpu.make_async_remote_copy(
            src_ref=outgoing.at[source], dst_ref=arrived.at[source],
            send_sem=cell_send.at[o], recv_sem=cell_recv.at[source],
            device_id=(source, d), device_id_type=MESH,
        ).wait_recv()
    there = [
        [home(positions_ref[(s * columns + d) * tiles + t]) for t in range(tiles)]
        for s in range(groups)
    ]
    slots = [
        pick((band == g, slot) for band, slot in there[s]) for s in range(groups)
    ]
    origin = [
        pick((slots[s] == j, s) for s in range(groups)) for j in range(tiles)
    ]
    for block in range(blocks):
        kind = 0 if block == 0 else 2 if block == blocks - 1 else 1
        total = None
        for row in range(ROWS):
            span = slice(row * COLS + block * BLOCK, row * COLS + (block + 1) * BLOCK)
            dark = dark_ref[:, span].astype(jnp.float32)
            inverse = inverse_ref[:, span]
            made = [
                ((arrived[origin[j], :, span].astype(jnp.float32) - dark) * inverse)
                .astype(jnp.bfloat16) for j in range(tiles)
            ]
            part = jnp.dot(
                jnp.concatenate(made, axis=0), weights[kind], preferred_element_type=jnp.float32
            )
            total = part if total is None else total + part
        lanes = slice(block * LANES, (block + 1) * LANES)
        total = total.astype(jnp.bfloat16).astype(jnp.float32)
        for j in range(tiles):
            placed[j, :, lanes] = total[j * planes:(j + 1) * planes]
    for j in range(tiles):
        cell = placed[j]
        base, shift = divmod(j * half_step, LANES)
        base = base * LANES
        if shift:
            cell = jnp.concatenate([cell, jnp.zeros((planes, LANES), jnp.float32)], axis=1)
            cell = pltpu.roll(cell, shift, 1)
        acc[:, base:base + cell.shape[1]] += cell

    @pl.when(d > 0)
    def _():
        spill = jnp.zeros((planes, LANES), jnp.float32)
        for o in range(groups):
            source = lax.rem(g + groups - o, groups)
            pltpu.make_async_remote_copy(
                src_ref=tail_out.at[source], dst_ref=tail_in.at[source],
                send_sem=tail_send.at[o], recv_sem=tail_recv.at[source],
                device_id=(source, lax.rem(d + columns - 1, columns)), device_id_type=MESH,
            ).wait_recv()
        before = [
            [home(positions_ref[(s * columns + d - 1) * tiles + t]) for t in range(tiles)]
            for s in range(groups)
        ]
        final = pick(
            ((band == g) & (slot == tiles - 1), s)
            for s in range(groups) for band, slot in before[s]
        )
        for row in range(ROWS):
            span = slice((row + 1) * COLS - OVL, (row + 1) * COLS)
            fixed = (
                (tail_in[final, row].astype(jnp.float32) - dark_ref[:, span].astype(jnp.float32))
                * inverse_ref[:, span]
            ).astype(jnp.bfloat16)
            spill = spill + jnp.dot(
                fixed, weights[2, BLOCK - OVL:, :], preferred_element_type=jnp.float32
            )
        spill = spill.astype(jnp.bfloat16).astype(jnp.float32)
        spill = pltpu.roll(spill, half_ovl, 1)
        lane = lax.broadcasted_iota(jnp.int32, (planes, LANES), 1)
        acc[:, 0:LANES] += jnp.where(lane < half_ovl, spill, 0.0)

    pooled_ref[...] = acc[:, 0:tiles * half_step].astype(jnp.bfloat16)
    for copy in sent:
        copy.wait_send()
    for copy in stores:
        copy.wait()
    for o in range(1, groups):
        cell_copy(o).wait_send()

    @pl.when(d < columns - 1)
    def _():
        for o in range(groups):
            tail_copy(o).wait_send()


def deliver(corrected_ref, pooled_ref, corrected_out, pooled_out, sems):
    tiles = corrected_ref.shape[0]
    copies = [pltpu.make_async_copy(pooled_ref, pooled_out, sems.at[tiles])]
    for t in range(tiles):
        copies.append(pltpu.make_async_copy(corrected_ref.at[t], corrected_out.at[t], sems.at[t]))
    for copy in copies:
        copy.start()
    for copy in copies:
        copy.wait()


def per_device(groups, columns, raw, dark, basis, counts, positions):
    tiles, planes, pixels = raw.shape
    half_step = (COLS - OVL) // 2
    bf16, f32 = jnp.bfloat16, jnp.float32
    vmem = pl.BlockSpec(memory_space=pltpu.VMEM)
    anywhere = pl.BlockSpec(memory_space=pl.ANY)
    dma = pltpu.SemaphoreType.DMA
    corrected, pooled = pl.pallas_call(
        functools.partial(kernel, groups, columns),
        out_shape=(
            jax.ShapeDtypeStruct(raw.shape, bf16),
            jax.ShapeDtypeStruct((planes, tiles * half_step), bf16),
        ),
        in_specs=[anywhere] * 5,
        out_specs=(anywhere, vmem),
        scratch_shapes=[
            pltpu.SMEM(counts.shape, jnp.int32),
            pltpu.SMEM(positions.shape, jnp.int32),
            pltpu.VMEM(raw.shape, bf16),
            pltpu.VMEM(dark.shape, bf16),
            pltpu.VMEM((16, pixels), bf16),
            pltpu.VMEM(raw.shape, bf16),
            pltpu.VMEM((planes, LANES), f32),
            pltpu.VMEM((groups, planes // 2, LANES), f32),
            pltpu.VMEM((columns, planes // 2, LANES), f32),
            pltpu.VMEM((3, BLOCK, LANES), bf16),
            pltpu.VMEM((groups, planes, pixels), bf16),
            pltpu.VMEM((groups, planes, pixels), bf16),
            pltpu.VMEM((groups, ROWS, planes, OVL), bf16),
            pltpu.VMEM((groups, ROWS, planes, OVL), bf16),
            pltpu.VMEM((planes, pixels), f32),
            pltpu.VMEM((tiles, planes, COLS // 2), f32),
            pltpu.VMEM((planes, tiles * half_step + LANES), f32),
            pltpu.VMEM(raw.shape, f32),
            pltpu.VMEM((3 * basis.shape[0], pixels), bf16),
            dma((4,)), dma((1,)), dma((1,)),
            dma((groups,)), dma((groups,)), dma((columns,)), dma((columns,)),
            dma((groups,)), dma((groups,)), dma((groups,)), dma((groups,)),
        ],
        compiler_params=pltpu.CompilerParams(
            collective_id=0, has_side_effects=True, vmem_limit_bytes=24 << 20
        ),
    )(*[pltpu.with_memory_space_constraint(x, pltpu.HBM) for x in (counts, positions, raw, dark, basis)])
    corrected, pooled = pl.pallas_call(
        deliver,
        out_shape=(
            jax.ShapeDtypeStruct(corrected.shape, bf16),
            jax.ShapeDtypeStruct(pooled.shape, bf16),
        ),
        in_specs=[anywhere] * 2,
        out_specs=(anywhere, anywhere),
        scratch_shapes=[dma((tiles + 1,))],
        compiler_params=pltpu.CompilerParams(vmem_limit_bytes=1 << 20),
    )(corrected, pooled)
    return corrected, pooled.reshape(1, planes, ROWS // 2, tiles * half_step)


def solution(mesh):
    in_specs = (P(("grp", "dev"), None, None), P(), P(), P(("grp", "dev")), P())
    out_specs = (P(("grp", "dev"), None, None), P("grp", None, None, "dev"))
    return jax.shard_map(
        functools.partial(per_device, mesh.shape["grp"], mesh.shape["dev"]),
        mesh=mesh, in_specs=in_specs, out_specs=out_specs, check_vma=False,
    )
```

```python
import functools

import jax
import jax.numpy as jnp
from jax import lax
from jax.experimental import pallas as pl
from jax.experimental.pallas import tpu as pltpu
from jax.sharding import PartitionSpec as P

ROWS = 2
COLS = 2048
OVL = 128
LANES = 128
BLOCK = 256
MESH = pl.DeviceIdType.MESH
NT = (((1,), (1,)), ((), ()))


def pick(options):
    found = jnp.int32(0)
    for hit, value in options:
        found = jnp.where(hit, value, found)
    return found


def pool_weights(block, blocks):
    row = lax.broadcasted_iota(jnp.int32, (BLOCK, LANES), 0)
    lane = lax.broadcasted_iota(jnp.int32, (BLOCK, LANES), 1)
    column = (row + block * BLOCK).astype(jnp.float32) + 0.5
    ramp = jnp.minimum(1.0, jnp.minimum(column / OVL, (blocks * BLOCK - column) / OVL))
    inside = (row >= 2 * lane) & (row < 2 * lane + 2)
    return jnp.where(inside, 0.25 * ramp, 0.0).astype(jnp.bfloat16)


def kernel(
    groups, columns,
    counts_hbm, positions_hbm, raw_hbm, dark_hbm, basis_hbm,
    corrected_hbm, pooled_ref,
    counts_ref, positions_ref, raw_ref, dark_ref, rhs, corrected_ref,
    stat, grp_buf, dev_buf, weights, outgoing, arrived, tail_out, tail_in, inverse_ref, placed, acc, diff, stack,
    in_sem, raw_sem, out_sem,
    grp_send, grp_recv, dev_send, dev_recv, cell_send, cell_recv, tail_send, tail_recv,
):
    tiles, planes, pixels = raw_ref.shape
    rank = basis_hbm.shape[0]
    band_size = columns * tiles
    half_step = (COLS - OVL) // 2
    half_ovl = OVL // 2
    blocks = COLS // BLOCK
    g = lax.axis_index("grp")
    d = lax.axis_index("dev")

    raw_loads = [pltpu.make_async_copy(raw_hbm, raw_ref, raw_sem.at[0])]
    loads = [
        pltpu.make_async_copy(basis_hbm, rhs.at[0:rank], in_sem.at[0]),
        pltpu.make_async_copy(dark_hbm, dark_ref, in_sem.at[1]),
        pltpu.make_async_copy(counts_hbm, counts_ref, in_sem.at[2]),
        pltpu.make_async_copy(positions_hbm, positions_ref, in_sem.at[3]),
    ]
    for copy in loads[:2] + raw_loads + loads[2:]:
        copy.start()

    barrier = pltpu.get_barrier_semaphore()
    near = [lax.rem(d + 1, columns), lax.rem(d + columns - 1, columns)]
    for o in range(1, groups):
        other = lax.rem(g + o, groups)
        for where in [d] + near:
            pl.semaphore_signal(barrier, inc=1, device_id=(other, where), device_id_type=MESH)
    for o in range(1, columns):
        pl.semaphore_signal(
            barrier, inc=1, device_id=(g, lax.rem(d + o, columns)), device_id_type=MESH
        )

    rhs[rank:, :] = jnp.ones((rhs.shape[0] - rank, pixels), jnp.bfloat16)
    width = rhs.shape[0]
    weights[0] = pool_weights(0, blocks)
    weights[1] = pool_weights(1, blocks)
    weights[2] = pool_weights(blocks - 1, blocks)
    stat[...] = jnp.zeros_like(stat)
    for copy in loads:
        copy.wait()
    dark_sums = lax.dot_general(dark_ref[...], rhs[...], NT, preferred_element_type=jnp.float32)
    plane = lax.broadcasted_iota(jnp.int32, (planes, width), 0)
    for copy in raw_loads:
        copy.wait()
    sums = lax.dot_general(
        raw_ref[...].reshape(tiles * planes, pixels), rhs[...], NT,
        preferred_element_type=jnp.float32,
    )
    local = jnp.zeros((planes, width), jnp.float32)
    for t in range(tiles):
        part = sums[t * planes:(t + 1) * planes] - dark_sums
        local = local + jnp.where(plane < counts_ref[t], part, 0.0)
    stat[:, 0:width] = local
    half = planes // 2
    grp_buf[g] = stat[0:half, :] + pltpu.roll(stat[half:, :], LANES // 2, 1)

    pl.semaphore_wait(barrier, 3 * (groups - 1) + columns - 1)

    sent = []
    for o in range(1, groups):
        other = lax.rem(g + o, groups)
        copy = pltpu.make_async_remote_copy(
            src_ref=grp_buf.at[g], dst_ref=grp_buf.at[g],
            send_sem=grp_send.at[o], recv_sem=grp_recv.at[g],
            device_id=(other, d), device_id_type=MESH,
        )
        copy.start()
        sent.append(copy)

    def home(at):
        return lax.div(at, band_size), lax.rem(at, tiles)

    wide = lax.broadcasted_iota(jnp.int32, (planes, pixels), 0)
    mine = [home(positions_ref[(g * columns + d) * tiles + t]) for t in range(tiles)]
    def build(b):
        chosen = pick((mine[t][0] == b, t) for t in range(tiles))
        masked = jnp.where(
            wide < counts_ref[chosen],
            raw_ref[chosen].astype(jnp.float32), dark_ref[...].astype(jnp.float32),
        ).astype(jnp.bfloat16)
        outgoing[b] = masked
        for row in range(ROWS):
            tail_out[b, row] = masked[:, (row + 1) * COLS - OVL:(row + 1) * COLS]

    def cell_copy(o):
        other = lax.rem(g + o, groups)
        return pltpu.make_async_remote_copy(
            src_ref=outgoing.at[other], dst_ref=arrived.at[g],
            send_sem=cell_send.at[o], recv_sem=cell_recv.at[g],
            device_id=(other, d), device_id_type=MESH,
        )

    def tail_copy(o):
        other = lax.rem(g + o, groups)
        return pltpu.make_async_remote_copy(
            src_ref=tail_out.at[other], dst_ref=tail_in.at[g],
            send_sem=tail_send.at[o], recv_sem=tail_recv.at[g],
            device_id=(other, lax.rem(d + 1, columns)), device_id_type=MESH,
        )

    for o in range(1, groups):
        build(lax.rem(g + o, groups))
        cell_copy(o).start()
    build(g)
    arrived[g] = outgoing[g]

    @pl.when(d < columns - 1)
    def _():
        for o in range(groups):
            tail_copy(o).start()

    for i in range(3):
        stack[i * rank:(i + 1) * rank, :] = rhs[0:rank, :]
    for t in range(tiles):
        bare = raw_ref[t].astype(jnp.float32) - dark_ref[...].astype(jnp.float32)
        diff[t] = jnp.where(wide < counts_ref[t], bare, 0.0)
    for o in range(1, groups):
        source = lax.rem(g + groups - o, groups)
        pltpu.make_async_remote_copy(
            src_ref=grp_buf.at[source], dst_ref=grp_buf.at[source],
            send_sem=grp_send.at[o], recv_sem=grp_recv.at[source],
            device_id=(source, d), device_id_type=MESH,
        ).wait_recv()
    dev_buf[d] = jnp.sum(grp_buf[...], axis=0)
    for o in range(1, columns):
        copy = pltpu.make_async_remote_copy(
            src_ref=dev_buf.at[d], dst_ref=dev_buf.at[d],
            send_sem=dev_send.at[o], recv_sem=dev_recv.at[d],
            device_id=(g, lax.rem(d + o, columns)), device_id_type=MESH,
        )
        copy.start()
        sent.append(copy)
    acc[...] = jnp.zeros_like(acc)
    for o in range(1, columns):
        source = lax.rem(d + columns - o, columns)
        pltpu.make_async_remote_copy(
            src_ref=dev_buf.at[source], dst_ref=dev_buf.at[source],
            send_sem=dev_send.at[o], recv_sem=dev_recv.at[source],
            device_id=(g, source), device_id_type=MESH,
        ).wait_recv()
    packed = jnp.sum(dev_buf[...], axis=0)
    full = jnp.concatenate([packed, pltpu.roll(packed, LANES // 2, 1)], axis=0)
    coef = full[:, 0:rank] / full[:, rank:rank + 1]
    high = coef.astype(jnp.bfloat16)
    rest = coef - high.astype(jnp.float32)
    middle = rest.astype(jnp.bfloat16)
    low = (rest - middle.astype(jnp.float32)).astype(jnp.bfloat16)

    parts = jnp.concatenate([low, middle, high], axis=1)
    for block in range(pixels // BLOCK):
        span = slice(block * BLOCK, (block + 1) * BLOCK)
        shade = jnp.dot(parts, stack[:, span], preferred_element_type=jnp.float32)
        inverse = jnp.exp(-shade)
        inverse_ref[:, span] = inverse
        for t in range(tiles):
            corrected_ref[t, :, span] = (diff[t, :, span] * inverse).astype(jnp.bfloat16)

    stores = [pltpu.make_async_copy(corrected_ref, corrected_hbm, out_sem.at[0])]
    for copy in stores:
        copy.start()
    for o in range(1, groups):
        source = lax.rem(g + groups - o, groups)
        pltpu.make_async_remote_copy(
            src_ref=outgoing.at[source], dst_ref=arrived.at[source],
            send_sem=cell_send.at[o], recv_sem=cell_recv.at[source],
            device_id=(source, d), device_id_type=MESH,
        ).wait_recv()
    there = [
        [home(positions_ref[(s * columns + d) * tiles + t]) for t in range(tiles)]
        for s in range(groups)
    ]
    slots = [
        pick((band == g, slot) for band, slot in there[s]) for s in range(groups)
    ]
    origin = [
        pick((slots[s] == j, s) for s in range(groups)) for j in range(tiles)
    ]
    for block in range(blocks):
        kind = 0 if block == 0 else 2 if block == blocks - 1 else 1
        total = None
        for row in range(ROWS):
            span = slice(row * COLS + block * BLOCK, row * COLS + (block + 1) * BLOCK)
            dark = dark_ref[:, span].astype(jnp.float32)
            inverse = inverse_ref[:, span]
            made = [
                ((arrived[origin[j], :, span].astype(jnp.float32) - dark) * inverse)
                .astype(jnp.bfloat16) for j in range(tiles)
            ]
            part = jnp.dot(
                jnp.concatenate(made, axis=0), weights[kind], preferred_element_type=jnp.float32
            )
            total = part if total is None else total + part
        lanes = slice(block * LANES, (block + 1) * LANES)
        total = total.astype(jnp.bfloat16).astype(jnp.float32)
        for j in range(tiles):
            placed[j, :, lanes] = total[j * planes:(j + 1) * planes]
    for j in range(tiles):
        cell = placed[j]
        base, shift = divmod(j * half_step, LANES)
        base = base * LANES
        if shift:
            cell = jnp.concatenate([cell, jnp.zeros((planes, LANES), jnp.float32)], axis=1)
            cell = pltpu.roll(cell, shift, 1)
        acc[:, base:base + cell.shape[1]] += cell

    @pl.when(d > 0)
    def _():
        spill = jnp.zeros((planes, LANES), jnp.float32)
        for o in range(groups):
            source = lax.rem(g + groups - o, groups)
            pltpu.make_async_remote_copy(
                src_ref=tail_out.at[source], dst_ref=tail_in.at[source],
                send_sem=tail_send.at[o], recv_sem=tail_recv.at[source],
                device_id=(source, lax.rem(d + columns - 1, columns)), device_id_type=MESH,
            ).wait_recv()
        before = [
            [home(positions_ref[(s * columns + d - 1) * tiles + t]) for t in range(tiles)]
            for s in range(groups)
        ]
        final = pick(
            ((band == g) & (slot == tiles - 1), s)
            for s in range(groups) for band, slot in before[s]
        )
        for row in range(ROWS):
            span = slice((row + 1) * COLS - OVL, (row + 1) * COLS)
            fixed = (
                (tail_in[final, row].astype(jnp.float32) - dark_ref[:, span].astype(jnp.float32))
                * inverse_ref[:, span]
            ).astype(jnp.bfloat16)
            spill = spill + jnp.dot(
                fixed, weights[2, BLOCK - OVL:, :], preferred_element_type=jnp.float32
            )
        spill = spill.astype(jnp.bfloat16).astype(jnp.float32)
        spill = pltpu.roll(spill, half_ovl, 1)
        lane = lax.broadcasted_iota(jnp.int32, (planes, LANES), 1)
        acc[:, 0:LANES] += jnp.where(lane < half_ovl, spill, 0.0)

    pooled_ref[...] = acc[:, 0:tiles * half_step].astype(jnp.bfloat16)
    for copy in sent:
        copy.wait_send()
    for copy in stores:
        copy.wait()
    for o in range(1, groups):
        cell_copy(o).wait_send()

    @pl.when(d < columns - 1)
    def _():
        for o in range(groups):
            tail_copy(o).wait_send()


def deliver(corrected_ref, pooled_ref, corrected_out, pooled_out, sems):
    tiles = corrected_ref.shape[0]
    copies = [pltpu.make_async_copy(pooled_ref, pooled_out, sems.at[tiles])]
    for t in range(tiles):
        copies.append(pltpu.make_async_copy(corrected_ref.at[t], corrected_out.at[t], sems.at[t]))
    for copy in copies:
        copy.start()
    for copy in copies:
        copy.wait()


def per_device(groups, columns, raw, dark, basis, counts, positions):
    tiles, planes, pixels = raw.shape
    half_step = (COLS - OVL) // 2
    bf16, f32 = jnp.bfloat16, jnp.float32
    vmem = pl.BlockSpec(memory_space=pltpu.VMEM)
    anywhere = pl.BlockSpec(memory_space=pl.ANY)
    dma = pltpu.SemaphoreType.DMA
    corrected, pooled = pl.pallas_call(
        functools.partial(kernel, groups, columns),
        out_shape=(
            jax.ShapeDtypeStruct(raw.shape, bf16),
            jax.ShapeDtypeStruct((planes, tiles * half_step), bf16),
        ),
        in_specs=[anywhere] * 5,
        out_specs=(anywhere, vmem),
        scratch_shapes=[
            pltpu.SMEM(counts.shape, jnp.int32),
            pltpu.SMEM(positions.shape, jnp.int32),
            pltpu.VMEM(raw.shape, bf16),
            pltpu.VMEM(dark.shape, bf16),
            pltpu.VMEM((16, pixels), bf16),
            pltpu.VMEM(raw.shape, bf16),
            pltpu.VMEM((planes, LANES), f32),
            pltpu.VMEM((groups, planes // 2, LANES), f32),
            pltpu.VMEM((columns, planes // 2, LANES), f32),
            pltpu.VMEM((3, BLOCK, LANES), bf16),
            pltpu.VMEM((groups, planes, pixels), bf16),
            pltpu.VMEM((groups, planes, pixels), bf16),
            pltpu.VMEM((groups, ROWS, planes, OVL), bf16),
            pltpu.VMEM((groups, ROWS, planes, OVL), bf16),
            pltpu.VMEM((planes, pixels), f32),
            pltpu.VMEM((tiles, planes, COLS // 2), f32),
            pltpu.VMEM((planes, tiles * half_step + LANES), f32),
            pltpu.VMEM(raw.shape, f32),
            pltpu.VMEM((3 * basis.shape[0], pixels), bf16),
            dma((4,)), dma((1,)), dma((1,)),
            dma((groups,)), dma((groups,)), dma((columns,)), dma((columns,)),
            dma((groups,)), dma((groups,)), dma((groups,)), dma((groups,)),
        ],
        compiler_params=pltpu.CompilerParams(
            collective_id=0, has_side_effects=True, vmem_limit_bytes=24 << 20
        ),
    )(*[pltpu.with_memory_space_constraint(x, pltpu.HBM) for x in (counts, positions, raw, dark, basis)])
    corrected, pooled = pl.pallas_call(
        deliver,
        out_shape=(
            jax.ShapeDtypeStruct(corrected.shape, bf16),
            jax.ShapeDtypeStruct(pooled.shape, bf16),
        ),
        in_specs=[anywhere] * 2,
        out_specs=(anywhere, anywhere),
        scratch_shapes=[dma((tiles + 1,))],
        compiler_params=pltpu.CompilerParams(vmem_limit_bytes=1 << 20),
    )(corrected, pooled)
    return corrected, pooled.reshape(1, planes, ROWS // 2, tiles * half_step)


def solution(mesh):
    in_specs = (P(("grp", "dev"), None, None), P(), P(), P(("grp", "dev")), P())
    out_specs = (P(("grp", "dev"), None, None), P("grp", None, None, "dev"))
    return jax.shard_map(
        functools.partial(per_device, mesh.shape["grp"], mesh.shape["dev"]),
        mesh=mesh, in_specs=in_specs, out_specs=out_specs, check_vma=False,
    )
```
